128 devices in a mesh: dp: 8 (over y, core), mp: 16 (over x, z).
Axes of the slice: x: 4, y: 4, z: 4, core: 2. Of those that a mesh axis runs over, the one named last changes fastest.
Arguments:
- span_tokens: bfloat16 [128, 256, 2560], P(('dp', 'mp')), may hold values from -6 to 6
- decode_tokens: bfloat16 [256, 2560], P(('dp', 'mp')), may hold values from -6 to 6
- norm_gain: float32 [2560], replicated, may hold values from 0.5 to 1.5
- query_weight: bfloat16 [2560, 2560], P(('dp', 'mp')), may hold values from -0.125 to 0.125
- keyval_weight: bfloat16 [2560, 512], P(('dp', 'mp')), may hold values from -0.125 to 0.125
- output_weight: bfloat16 [2560, 2560], P(('dp', 'mp')), may hold values from -0.125 to 0.125
- span_cache: bfloat16 [128, 2048, 512], P(('dp', 'mp')), may hold values from -360 to 360
- decode_cache: bfloat16 [256, 2048, 512], P(('dp', 'mp')), may hold values from -360 to 360
- span_index: int32 [128], P(('dp', 'mp')), may hold values from 0 to 15
- decode_length: int32 [256], P(('dp', 'mp')), may hold values from 1 to 32768
- cache_slot: int32 [256], replicated, may hold values from 0 to 255, each once
Outputs:
- span_output: bfloat16 [128, 256, 2560], P(('dp', 'mp'))
- span_keyval: bfloat16 [128, 256, 512], P(('dp', 'mp'))
- decode_output: bfloat16 [256, 2560], P(('dp', 'mp'))
- decode_keyval: bfloat16 [256, 512], P(('dp', 'mp'))
The draws below stay inside these ranges and needn't reach their ends.
Inputs may be any that keep to these rules, and one draw needn't show every extreme that they name: `cache_slot`: each cache slot belongs to exactly one request.
All inputs are finite; a program needn't handle non-finite values.
Results may differ from the reference program's by a relative error of at most 0.024.
Values may be sent and summed in bfloat16 or wider, within the bound.
No kernel may reach another device: no remote copies, remote signals or barrier semaphores. Data moves between devices by JAX's collectives and lax.ppermute only.
A program may use at most 128 MiB of HBM per device.

```python
import jax
import jax.numpy as jnp
from jax import lax

D = 2560
H = 10
HD = 256
W = 2048
C = 256
NCHUNK = 128
NDEC = 256


def cache_values(seed_key, dims):
    normal_part = jax.random.truncated_normal(seed_key, -6.0, 6.0, dims, jnp.float32)
    return normal_part.astype(jnp.bfloat16)


def draw_span_cache(key, part):
    return cache_values(jax.random.fold_in(key, 3), (NCHUNK, W, 2 * HD))


def draw_decode_cache(key, part):
    return cache_values(jax.random.fold_in(key, 5), (NDEC, W, 2 * HD))


def set_ends(array, rng, least, largest):
    place = [jax.random.randint(jax.random.fold_in(rng, axis), (), 0, length) for axis, length in enumerate(array.shape)]
    main_axis = array.shape.index(max(array.shape))
    beside = place[:main_axis] + [(place[main_axis] + 1) % array.shape[main_axis]] + place[main_axis + 1:]
    return array.at[tuple(place)].set(least).at[tuple(beside)].set(largest)


def block_scale(rng, shape, split, least, high):
    gain = 1.0
    for axis_at, blocks in split:
        heights = jax.random.uniform(jax.random.fold_in(jax.random.fold_in(rng, 6), axis_at), (blocks,), jnp.float32, least / len(split), high / len(split))
        gain = gain * jnp.repeat(jnp.exp(heights), shape[axis_at] // blocks).reshape((-1,) + (1,) * (len(shape) - 1 - axis_at))
    return gain


def normal_values(rng, extent, scale, reach, shards=(), held_as=jnp.bfloat16):
    result = jax.random.normal(rng, extent, jnp.float32) * scale
    if len(shards) > 0:
        result = block_scale(rng, extent, shards, -0.22, 0.18) * result
    return jnp.clip(result, min=-reach, max=reach).astype(held_as)


def setup_inputs(seed: int = 0) -> dict:
    key_of = jax.random.split(jax.random.key(seed), 12)
    return {
        "span_tokens": normal_values(key_of[0], (NCHUNK, C, D), 1.0, 6.0, ((0, 128),)),
        "decode_tokens": normal_values(key_of[1], (NDEC, D), 1.0, 6.0, ((0, 128),)),
        "norm_gain": jnp.clip(1.0 + 0.1 * jax.random.normal(key_of[2], (D,), jnp.float32), 0.5, 1.5),
        "query_weight": normal_values(key_of[3], (D, H * HD), D ** -0.5, 0.125, ((0, 128),)),
        "keyval_weight": normal_values(key_of[4], (D, 2 * HD), D ** -0.5, 0.125, ((0, 128),)),
        "output_weight": normal_values(key_of[5], (H * HD, D), (H * HD) ** -0.5, 0.125, ((0, 128),)),
        "span_cache": draw_span_cache(jax.random.fold_in(key_of[11], 71), 0),
        "decode_cache": draw_decode_cache(jax.random.fold_in(key_of[11], 71), 0),
        "span_index": set_ends(jax.random.randint(key_of[8], (NCHUNK,), 0, 16), jax.random.fold_in(key_of[8], 1), 0, 15).astype(jnp.int32),
        "decode_length": set_ends(jax.random.randint(key_of[9], (NDEC,), 1, 32769), jax.random.fold_in(key_of[9], 1), 1, 32768).astype(jnp.int32),
        "cache_slot": jax.random.permutation(key_of[10], NDEC).astype(jnp.int32),
    }


def rms_normed(rows_in, norm_gain):
    widened = rows_in.astype(jnp.float32)
    spread = lax.optimization_barrier(jnp.mean(widened * widened, axis=-1, keepdims=True))
    return (widened * lax.rsqrt(spread + 1e-06) * norm_gain).astype(jnp.bfloat16)

def rotate(values, positions):
    quarter = values.shape[-1] // 4
    frequency = 10000.0 ** (-jnp.arange(quarter, dtype=jnp.float32) / quarter)
    angles = positions.astype(jnp.float32)[..., None] * frequency
    cos_part = jnp.cos(angles)
    sin_part = jnp.sin(angles)
    first_half = values[..., :quarter]
    second_half = values[..., quarter:2 * quarter]
    return jnp.concatenate([first_half * cos_part - second_half * sin_part, second_half * cos_part + first_half * sin_part, values[..., 2 * quarter:]], -1)

def project(rows_in, norm_gain, query_weight, keyval_weight, positions):
    normed = rms_normed(rows_in, norm_gain)
    row_count = rows_in.shape[0]
    query_all = jnp.dot(normed, query_weight, preferred_element_type=jnp.float32)
    keyval_all = jnp.dot(normed, keyval_weight, preferred_element_type=jnp.float32)
    queries = rotate(query_all.reshape(row_count, H, HD), positions[:, None]).astype(jnp.bfloat16)
    key_rows = rotate(keyval_all[:, :HD], positions).astype(jnp.bfloat16)
    keyval = jnp.concatenate([key_rows, keyval_all[:, HD:].astype(jnp.bfloat16)], 1)
    return (queries, keyval)

def span_attend(queries, keyval, stored, offset):
    length = queries.shape[0]
    window = stored.shape[0]
    key_rows = jnp.concatenate([stored[:, :HD], keyval[:, :HD]], 0).astype(jnp.float32)
    value_rows = jnp.concatenate([stored[:, HD:], keyval[:, HD:]], 0).astype(jnp.float32)
    scores = jnp.einsum('chd,kd->chk', queries.astype(jnp.float32), key_rows) * HD ** (-0.5)
    row_ids = jnp.arange(length, dtype=jnp.int32)
    slot_ids = jnp.arange(window, dtype=jnp.int32)
    held_pos = offset - 1 - jnp.mod(offset - 1 - slot_ids, window)
    cache_ok = (held_pos[None, :] >= 0) & (held_pos[None, :] >= offset + row_ids[:, None] - window + 1)
    own_ok = row_ids[None, :] <= row_ids[:, None]
    allowed = jnp.concatenate([cache_ok, own_ok], 1)[:, None, :]
    highest = lax.optimization_barrier(jnp.max(jnp.where(allowed, scores, -1e+30), -1, keepdims=True))
    exp_terms = jnp.where(allowed, jnp.exp(scores - highest), 0.0)
    weights = (exp_terms / lax.optimization_barrier(jnp.sum(exp_terms, -1, keepdims=True))).astype(jnp.bfloat16)
    attended = jnp.einsum('chk,kd->chd', weights.astype(jnp.float32), value_rows)
    return attended.astype(jnp.bfloat16).reshape(length, -1)

def decode_attend(queries, keyval, stored, length):
    window = stored.shape[1]
    score_scale = HD ** (-0.5)
    exp_scores = jnp.einsum('ehd,ewd->ehw', queries.astype(jnp.float32), stored[..., :HD].astype(jnp.float32)) * score_scale
    self_scores = jnp.einsum('ehd,ed->eh', queries.astype(jnp.float32), keyval[:, :HD].astype(jnp.float32)) * score_scale
    slot_ids = jnp.arange(window, dtype=jnp.int32)
    allowed = (slot_ids[None, :] < length[:, None]) & (slot_ids[None, :] != jnp.mod(length, window)[:, None])
    allowed = allowed[:, None, :]
    highest = jnp.maximum(lax.optimization_barrier(jnp.max(jnp.where(allowed, exp_scores, -1e+30), -1)), self_scores)
    exp_cache = jnp.where(allowed, jnp.exp(exp_scores - highest[..., None]), 0.0)
    exp_self = jnp.exp(self_scores - highest)
    denominator = lax.optimization_barrier(jnp.sum(exp_cache, -1)) + exp_self
    weight_cache = (exp_cache / denominator[..., None]).astype(jnp.bfloat16)
    weight_self = (exp_self / denominator).astype(jnp.bfloat16)
    attended = jnp.einsum('ehw,ewd->ehd', weight_cache.astype(jnp.float32), stored[..., HD:].astype(jnp.float32))
    attended = attended + weight_self.astype(jnp.float32)[..., None] * keyval[:, None, HD:].astype(jnp.float32)
    return attended.astype(jnp.bfloat16).reshape(queries.shape[0], -1)

def finish(tokens, attended, output_weight):
    return (tokens.astype(jnp.float32) + jnp.dot(attended, output_weight, preferred_element_type=jnp.float32)).astype(jnp.bfloat16)

def reference(span_tokens, decode_tokens, norm_gain, query_weight, keyval_weight, output_weight, span_cache, decode_cache, span_index, decode_length, cache_slot):

    def one_span(packed):
        tokens, stored, span_number = packed
        offset = span_number * C
        positions = offset + jnp.arange(C, dtype=jnp.int32)
        queries, keyval = project(tokens, norm_gain, query_weight, keyval_weight, positions)
        attended = span_attend(queries, keyval, stored, offset)
        return (finish(tokens, attended, output_weight), keyval)
    span_output, span_keyval = lax.map(one_span, (span_tokens, span_cache, span_index))
    queries, keyval = project(decode_tokens, norm_gain, query_weight, keyval_weight, decode_length)

    def one_request(packed):
        query_one, keyval_one, length, slot_id = packed
        stored = lax.dynamic_index_in_dim(decode_cache, slot_id.astype(jnp.int32), 0, keepdims=True)
        return decode_attend(query_one[None], keyval_one[None], stored, length[None])[0]
    attended = lax.map(one_request, (queries, keyval, decode_length, cache_slot))
    decode_output = finish(decode_tokens, attended, output_weight)
    decode_keyval = jnp.zeros((NDEC, 2 * HD), jnp.bfloat16).at[cache_slot].set(keyval)
    return (span_output, span_keyval, decode_output, decode_keyval)
```

```python
import functools

import jax
import jax.numpy as jnp
import numpy as np
from jax import lax
from jax.experimental import pallas as pl
from jax.experimental.pallas import tpu as pltpu
from jax.sharding import PartitionSpec as P

AXES = ("dp", "mp")
LOG2E = 1.4426950408889634
NEG = -1e30
F32 = jnp.float32
BF16 = jnp.bfloat16
EXTRA = 16


def params(mib, *semantics):
    return pltpu.CompilerParams(vmem_limit_bytes=mib << 20, dimension_semantics=semantics or None)


def dot(a, b):
    return jnp.dot(a, b, preferred_element_type=F32)


def dot_t(a, b):
    return lax.dot_general(a, b, (((1,), (1,)), ((), ())), preferred_element_type=F32)


def spreader(run, padded, runs):
    src = np.arange(run * runs)
    to = (src // run) * padded + src % run
    return (jnp.asarray(to, jnp.int32)[:, None] == jnp.arange(padded * runs)[None, :]).astype(BF16)


def norm_body(x_ref, gain_ref, spread_ref, out_ref):
    x = x_ref[...].astype(F32)
    mean = jnp.mean(x * x, axis=-1, keepdims=True)
    normed = (x * lax.rsqrt(mean + 1e-06) * gain_ref[...]).astype(BF16)
    k, kp = spread_ref.shape
    for g in range(x.shape[1] // k):
        out_ref[:, g * kp : (g + 1) * kp] = dot(
            normed[:, g * k : (g + 1) * k], spread_ref[...]
        ).astype(BF16)


def norm_spread(x, gain, spread):
    rows, width = x.shape
    return pl.pallas_call(
        norm_body,
        out_shape=jax.ShapeDtypeStruct((rows, width // spread.shape[0] * spread.shape[1]), BF16),
        compiler_params=params(40),
        name="norm_spread",
    )(x, gain[None], spread)


def rotate(v, cos_ref, sin_ref):
    half = v[:, :128]
    turned = half * cos_ref[...] + pltpu.roll(half, 64, 1) * sin_ref[...]
    return jnp.concatenate([turned, v[:, 128:]], 1)


def project_body(last, x_ref, w_ref, cos_ref, sin_ref, out_ref):
    v = dot(x_ref[...], w_ref[...])

    @pl.when(pl.program_id(0) < last)
    def _():
        out_ref[0] = rotate(v, cos_ref, sin_ref).astype(BF16)

    @pl.when(pl.program_id(0) == last)
    def _():
        out_ref[0] = v.astype(BF16)


def project(x, w, cos, sin, hd):
    rows, depth = x.shape
    blocks = w.shape[1] // hd
    return pl.pallas_call(
        functools.partial(project_body, blocks - 1),
        grid=(blocks,),
        in_specs=[
            pl.BlockSpec((rows, depth), lambda i: (0, 0)),
            pl.BlockSpec((depth, hd), lambda i: (0, i)),
            pl.BlockSpec((rows, 128), lambda i: (0, 0)),
            pl.BlockSpec((rows, 128), lambda i: (0, 0)),
        ],
        out_specs=pl.BlockSpec((1, rows, hd), lambda i: (i, 0, 0)),
        out_shape=jax.ShapeDtypeStruct((blocks, rows, hd), BF16),
        compiler_params=params(40, "arbitrary"),
        cost_estimate=pl.CostEstimate(
            flops=2 * rows * depth * w.shape[1], bytes_accessed=2 * depth * w.shape[1], transcendentals=0
        ),
        name="project",
    )(x, w, cos, sin)


def decode_body(len_ref, q_ref, own_ref, cache_ref, out_ref):
    length = len_ref[pl.program_id(0)]
    q = q_ref[0]
    hd = q.shape[1]
    window = cache_ref.shape[1]
    scores = dot_t(q, cache_ref[0, :, :hd])
    own_key = own_ref[0, :, :hd].astype(F32)
    own = jnp.sum(q.astype(F32) * own_key, axis=1, keepdims=True)
    slot = lax.broadcasted_iota(jnp.int32, scores.shape, 1)
    met = (slot < length) & (slot != lax.rem(length, window))
    scores = jnp.where(met, scores, NEG)
    top = jnp.maximum(jnp.max(scores, 1, keepdims=True), own)
    scale = LOG2E * hd**-0.5
    terms = jnp.where(met, jnp.exp2((scores - top) * scale), 0.0)
    own_term = jnp.exp2((own - top) * scale)
    total = jnp.sum(terms, 1, keepdims=True) + own_term
    weights = (terms / total).astype(BF16)
    own_weight = (own_term / total).astype(BF16).astype(F32)
    mixed = dot(weights, cache_ref[0, :, hd:]) + own_weight * own_ref[0, :, hd:].astype(F32)
    out_ref[0] = mixed.astype(BF16)


def decode_attend(lengths, q, own, cache):
    n, heads, hd = q.shape
    window = cache.shape[1]
    return pl.pallas_call(
        decode_body,
        grid_spec=pltpu.PrefetchScalarGridSpec(
            num_scalar_prefetch=1,
            grid=(n,),
            in_specs=[
                pl.BlockSpec((1, heads, hd), lambda i, s: (i, 0, 0)),
                pl.BlockSpec((1, 1, 2 * hd), lambda i, s: (i, 0, 0)),
                pl.BlockSpec((1, window, 2 * hd), lambda i, s: (i, 0, 0)),
            ],
            out_specs=pl.BlockSpec((1, heads, hd), lambda i, s: (i, 0, 0)),
        ),
        out_shape=jax.ShapeDtypeStruct((n, heads, hd), BF16),
        compiler_params=params(32, "arbitrary"),
        cost_estimate=pl.CostEstimate(
            flops=4 * n * heads * hd * window, bytes_accessed=4 * n * hd * window, transcendentals=0
        ),
        name="decode_attend",
    )(lengths, q, own[:, None], cache)


def span_body(index_ref, q_ref, k_ref, v_ref, cache_ref, out_ref):
    index = index_ref[0]
    q = q_ref[0]
    rows, hd = q.shape
    blocks = cache_ref.shape[1] // rows
    wrapped = index >= blocks
    row = lax.broadcasted_iota(jnp.int32, (rows, rows), 0)
    col = lax.broadcasted_iota(jnp.int32, (rows, rows), 1)
    own = col <= row
    starts, scores, shifts = [], [], []
    top = None
    for rel in range(blocks):
        block = lax.rem(index + rel, blocks)
        start = pl.multiple_of(block * rows, rows)
        starts.append(start)
        s = dot_t(q, cache_ref[0, pl.ds(start, rows), :hd])
        if rel == 0:
            s = jnp.where(own, dot_t(q, k_ref[0]), jnp.where(wrapped, s, NEG))
            shift = jnp.float32(0)
        else:
            shift = jnp.where(wrapped | (block < index), jnp.float32(0), jnp.float32(NEG))
        scores.append(s)
        shifts.append(shift)
        peak = jnp.max(s, 1, keepdims=True) + shift
        top = peak if top is None else jnp.maximum(top, peak)
    scale = LOG2E * hd**-0.5
    base = top * scale
    total = jnp.zeros((rows, 1), F32)
    mixed = jnp.zeros((rows, hd), F32)
    for rel in range(blocks):
        terms = jnp.exp2(scores[rel] * scale - (base - shifts[rel]))
        total += jnp.sum(terms, 1, keepdims=True)
        old_values = cache_ref[0, pl.ds(starts[rel], rows), hd:]
        if rel == 0:
            mixed += dot(jnp.where(own, terms, 0.0).astype(BF16), v_ref[0])
            mixed += dot(jnp.where(own, 0.0, terms).astype(BF16), old_values)
        else:
            mixed += dot(terms.astype(BF16), old_values)
    out_ref[...] = (mixed / total).astype(BF16)


def span_attend(index, qkv, rows, cache):
    heads, hd = qkv.shape[0] - 2, qkv.shape[2]
    window = cache.shape[1]
    return pl.pallas_call(
        span_body,
        grid_spec=pltpu.PrefetchScalarGridSpec(
            num_scalar_prefetch=1,
            grid=(heads,),
            in_specs=[
                pl.BlockSpec((1, rows, hd), lambda h, s: (h, 0, 0)),
                pl.BlockSpec((1, rows, hd), lambda h, s: (heads, 0, 0)),
                pl.BlockSpec((1, rows, hd), lambda h, s: (heads + 1, 0, 0)),
                pl.BlockSpec((1, window, 2 * hd), lambda h, s: (0, 0, 0)),
            ],
            out_specs=pl.BlockSpec((rows, hd), lambda h, s: (0, h)),
        ),
        out_shape=jax.ShapeDtypeStruct((rows, heads * hd), BF16),
        compiler_params=params(48, "arbitrary"),
        cost_estimate=pl.CostEstimate(
            flops=4 * heads * rows * hd * (window + rows),
            bytes_accessed=4 * hd * window,
            transcendentals=heads * rows * window,
        ),
        name="span_attend",
    )(index, qkv, qkv, qkv, cache)


def finish_body(att_ref, datt_ref, x_ref, dx_ref, spread_ref, w_ref, out_ref, dout_ref, lhs):
    rows = att_ref.shape[0]
    k, kp = spread_ref.shape

    @pl.when(pl.program_id(0) == 0)
    def _():
        for g in range(att_ref.shape[1] // k):
            from_, to = slice(g * k, (g + 1) * k), slice(g * kp, (g + 1) * kp)
            lhs[:rows, to] = dot(att_ref[:, from_], spread_ref[...]).astype(BF16)
            lhs[rows:, to] = dot(datt_ref[:, from_], spread_ref[...]).astype(BF16)

    y = dot(lhs[...], w_ref[...])
    out_ref[...] = (x_ref[...].astype(F32) + y[:rows]).astype(BF16)
    dout_ref[...] = (dx_ref[...].astype(F32) + y[rows:]).astype(BF16)


def finish(att, datt, x, dx, spread, w):
    rows, width = x.shape
    drows = dx.shape[0]
    depth, n = w.shape
    bn = 512
    return pl.pallas_call(
        finish_body,
        grid=(n // bn,),
        in_specs=[
            pl.BlockSpec(att.shape, lambda i: (0, 0)),
            pl.BlockSpec(datt.shape, lambda i: (0, 0)),
            pl.BlockSpec((rows, bn), lambda i: (0, i)),
            pl.BlockSpec((drows, bn), lambda i: (0, i)),
            pl.BlockSpec(spread.shape, lambda i: (0, 0)),
            pl.BlockSpec((depth, bn), lambda i: (0, i)),
        ],
        out_specs=[
            pl.BlockSpec((rows, bn), lambda i: (0, i)),
            pl.BlockSpec((drows, bn), lambda i: (0, i)),
        ],
        out_shape=[
            jax.ShapeDtypeStruct((rows, n), BF16),
            jax.ShapeDtypeStruct((drows, n), BF16),
        ],
        scratch_shapes=[pltpu.VMEM((rows + drows, depth), BF16)],
        compiler_params=params(48, "arbitrary"),
        cost_estimate=pl.CostEstimate(
            flops=2 * rows * depth * n, bytes_accessed=2 * depth * n, transcendentals=0
        ),
        name="finish",
    )(att, datt, x, dx, spread, w)


def route(rows, to, devices):
    places = jnp.arange(devices * rows.shape[0], dtype=jnp.int32)
    sent = jnp.zeros((places.shape[0], rows.shape[1]), BF16)
    for i in range(rows.shape[0]):
        sent = jnp.where((places == to[i])[:, None], rows[i][None], sent)
    sent = sent.reshape(devices, rows.shape[0], rows.shape[1])
    return lax.all_to_all(sent, AXES, 0, 0)


def pick(arrived, came_from):
    each = arrived.shape[1]
    return jnp.concatenate(
        [
            lax.dynamic_slice(arrived, (came_from[i] // each, i, 0), (1, 1, arrived.shape[2]))[0]
            for i in range(each)
        ],
        0,
    )


def shards(
    devices,
    span_tokens,
    decode_tokens,
    norm_gain,
    query_weight,
    keyval_weight,
    output_weight,
    span_cache,
    decode_cache,
    span_index,
    decode_length,
    cache_slot,
):
    rows, width = span_tokens.shape[1:]
    own = decode_cache.shape[0]
    hd = keyval_weight.shape[1] // 2
    heads = query_weight.shape[1] // hd
    device = lax.axis_index(AXES)
    run = query_weight.shape[0]
    padded = -(-run // 8) * 8

    def gathered(w):
        return lax.all_gather(jnp.pad(w, ((0, padded - run), (0, 0))), AXES, axis=0, tiled=True)

    first_weight = gathered(jnp.concatenate([query_weight, keyval_weight], 1))
    spread = spreader(run, padded, 32)

    mine = device * own + jnp.arange(own, dtype=jnp.int32)
    slot_of_mine = lax.dynamic_slice_in_dim(cache_slot, device * own, own)
    request_of_mine = jnp.argmax(cache_slot[None, :] == mine[:, None], 1).astype(jnp.int32)
    digits = jnp.stack([decode_length // 256, decode_length % 256], 1).astype(BF16)
    tagged = jnp.concatenate([decode_tokens, jnp.pad(digits, ((0, 0), (0, 126)))], 1)
    arrived = pick(route(tagged, slot_of_mine, devices), request_of_mine)
    own_tokens = arrived[:, :width]
    tags = arrived[:, width : width + 2].astype(jnp.int32)
    own_length = tags[:, 0] * 256 + tags[:, 1]

    offset = span_index[0] * rows
    positions = jnp.concatenate(
        [offset + jnp.arange(rows, dtype=jnp.int32), own_length, jnp.zeros(EXTRA - own, jnp.int32)]
    )
    quarter = hd // 4
    frequency = 10000.0 ** (-jnp.arange(quarter, dtype=F32) / quarter)
    angles = positions.astype(F32)[:, None] * frequency
    cos, sin = jnp.cos(angles), jnp.sin(angles)
    cos = jnp.concatenate([cos, cos], 1)
    sin = jnp.concatenate([-sin, sin], 1)

    rows_all = jnp.concatenate([span_tokens[0], jnp.pad(own_tokens, ((0, EXTRA - own), (0, 0)))], 0)
    lhs = norm_spread(rows_all, norm_gain, spread)
    qkv = project(lhs, first_weight, cos, sin, hd)

    keyval = jnp.concatenate([qkv[heads], qkv[heads + 1]], 1)
    decode_keyval = keyval[rows : rows + own]
    decode_q = jnp.transpose(qkv[:heads, rows : rows + own], (1, 0, 2))
    decode_q = jnp.pad(decode_q, ((0, 0), (0, 16 - heads), (0, 0)))
    decode_mixed = decode_attend(own_length, decode_q, decode_keyval, decode_cache)
    decode_mixed = decode_mixed[:, :heads].reshape(own, width)
    home = route(decode_mixed, request_of_mine, devices)

    span_mixed = span_attend(span_index, qkv, rows, span_cache)
    home = jnp.pad(pick(home, slot_of_mine), ((0, EXTRA - own), (0, 0)))
    last_weight = gathered(output_weight)
    span_output, decode_output = finish(
        span_mixed,
        home,
        span_tokens[0],
        jnp.pad(decode_tokens, ((0, EXTRA - own), (0, 0))),
        spread,
        last_weight,
    )
    return span_output[None], keyval[:rows][None], decode_output[:own], decode_keyval


def solution(mesh):
    both = P(AXES)
    return jax.shard_map(
        functools.partial(shards, mesh.size),
        mesh=mesh,
        in_specs=(both, both, P(), both, both, both, both, both, both, both, P()),
        out_specs=(both, both, both, both),
        check_vma=False,
    )
```

```python
import functools

import jax
import jax.numpy as jnp
import numpy as np
from jax import lax
from jax.experimental import pallas as pl
from jax.experimental.pallas import tpu as pltpu
from jax.sharding import Mesh
from jax.sharding import PartitionSpec as P

AXES = ("y", "c", "x", "z")
CHIPS = ("y", "x", "z")
LOG2E = 1.4426950408889634
NEG = -1e30
F32 = jnp.float32
BF16 = jnp.bfloat16
EXTRA = 16


def params(mib, *semantics):
    return pltpu.CompilerParams(vmem_limit_bytes=mib << 20, dimension_semantics=semantics or None)


def dot(a, b):
    return jnp.dot(a, b, preferred_element_type=F32)


def dot_t(a, b):
    return lax.dot_general(a, b, (((1,), (1,)), ((), ())), preferred_element_type=F32)


def mover(to, width):
    return (jnp.asarray(to, jnp.int32)[:, None] == jnp.arange(width)[None, :]).astype(BF16)


def arrival_order(run):
    core, x, z, r = np.meshgrid(*(np.arange(n) for n in (2, 4, 4, run)), indexing="ij")
    return mover((((x * 4 + z) * 2 + core) * run + r).reshape(-1), 32 * run)


def norm_body(x_ref, gain_ref, order_ref, *refs):
    out_ref = refs[-1]
    x = x_ref[...].astype(F32)
    rows = x.shape[0]
    mean = jnp.mean(x * x, axis=-1, keepdims=True)
    normed = (x * lax.rsqrt(mean + 1e-06) * gain_ref[...]).astype(BF16)
    k = order_ref.shape[0]
    blocks = jnp.concatenate([normed[:, y * k : (y + 1) * k] for y in range(4)], 0)
    moved = dot(blocks, order_ref[...]).astype(BF16)
    for y in range(4):
        out_ref[:, y * k : (y + 1) * k] = moved[y * rows : (y + 1) * rows]


def norm_ordered(x, gain, order, total, block, at, into=()):
    rows, width = x.shape
    return pl.pallas_call(
        norm_body,
        grid=(rows // block,),
        in_specs=[
            pl.BlockSpec((block, width), lambda i: (i, 0)),
            pl.BlockSpec((1, width), lambda i: (0, 0)),
            pl.BlockSpec(order.shape, lambda i: (0, 0)),
        ]
        + [pl.BlockSpec(memory_space=pl.ANY)] * len(into),
        out_specs=pl.BlockSpec((block, width), lambda i: (at + i, 0)),
        out_shape=jax.ShapeDtypeStruct((total, width), BF16),
        input_output_aliases={3 + i: i for i in range(len(into))},
        compiler_params=params(24, "arbitrary"),
        cost_estimate=pl.CostEstimate(
            flops=2 * rows * width * 640, bytes_accessed=4 * rows * width, transcendentals=0
        ),
        name="norm_ordered",
    )(x, gain[None], order, *into)


def rotate(v, cos_ref, sin_ref):
    half = v[:, :128]
    turned = half * cos_ref[...] + pltpu.roll(half, 64, 1) * sin_ref[...]
    return jnp.concatenate([turned, v[:, 128:]], 1)


def project_body(rows, x_ref, w_ref, cos_ref, sin_ref, ours_ref, other_ref):
    extra = ours_ref.shape[1] - rows
    made = rotate(dot(x_ref[...], w_ref[...]), cos_ref.at[0], sin_ref.at[0]).astype(BF16)
    ours_ref[0, :rows] = made[:rows]
    other_ref[0, :rows] = made[rows : 2 * rows]
    ours_ref[0, rows:] = made[2 * rows : 2 * rows + extra]
    other_ref[0, rows:] = made[2 * rows + extra :]


def project(first, count, rows, x, w, cos, sin, hd):
    total, depth = x.shape
    last = w.shape[1] // hd - 1
    shape = jax.ShapeDtypeStruct((count, total // 2, hd), BF16)
    table = pl.BlockSpec((1, total, 128), lambda i: ((first + i) // last, 0, 0))
    return pl.pallas_call(
        functools.partial(project_body, rows),
        grid=(count,),
        in_specs=[
            pl.BlockSpec((total, depth), lambda i: (0, 0)),
            pl.BlockSpec((depth, hd), lambda i: (0, first + i)),
            table,
            table,
        ],
        out_specs=[pl.BlockSpec((1, total // 2, hd), lambda i: (i, 0, 0))] * 2,
        out_shape=[shape, shape],
        compiler_params=params(32, "arbitrary"),
        cost_estimate=pl.CostEstimate(
            flops=2 * total * count * depth * hd,
            bytes_accessed=2 * count * depth * hd,
            transcendentals=0,
        ),
        name="project",
    )(x, w, cos, sin)


SLAB = 24


def decode_body(
    info_ref, oab_ref, oc_ref, tab_ref, tc_ref, own_ref, cache_ref, out_ref, gather_ref, spill_ref
):
    i = pl.program_id(0)
    length, to, core = info_ref[i], info_ref[2 + i], info_ref[4]
    hd = cache_ref.shape[2] // 2
    window = cache_ref.shape[1]
    for half, (ab_ref, c_ref) in enumerate(((oab_ref, oc_ref), (tab_ref, tc_ref))):
        for h in range(5):
            block = ab_ref[h] if h < 4 else c_ref[0]
            block = block.astype(F32)
            row = jnp.where(i == 0, block[0:1], block[1:2])
            gather_ref[half * 5 + h : half * 5 + h + 1] = row
    gather_ref[10:16] = jnp.zeros((6, hd), F32)
    q = gather_ref[...].astype(BF16)
    scores = dot_t(q, cache_ref[0, :, :hd])
    own_row = own_ref[...].astype(F32)
    own_row = jnp.where(i == 0, own_row[0:1], own_row[1:2])
    own = jnp.sum(gather_ref[...] * own_row[:, :hd], axis=1, keepdims=True)
    slot = lax.broadcasted_iota(jnp.int32, scores.shape, 1)
    met = (slot < length) & (slot != lax.rem(length, window))
    scores = jnp.where(met, scores, NEG)
    top = jnp.maximum(jnp.max(scores, 1, keepdims=True), own)
    scale = LOG2E * hd**-0.5
    terms = jnp.where(met, jnp.exp2((scores - top) * scale), 0.0)
    own_term = jnp.exp2((own - top) * scale)
    total = jnp.sum(terms, 1, keepdims=True) + own_term
    weights = (terms / total).astype(BF16)
    own_weight = (own_term / total).astype(BF16).astype(F32)
    mixed = dot(weights, cache_ref[0, :, hd:]) + own_weight * own_row[:, hd:]
    spill_ref[20:] = jnp.zeros((SLAB - 20, 128), F32)
    for h in range(10):
        head = jnp.where(core == 0, h, (h + 5) % 10)
        for part in range(2):
            spill_ref[pl.ds(2 * head + part, 1)] = mixed[h : h + 1, part * 128 : part * 128 + 128]
    out_ref[to] = spill_ref[...].astype(BF16)


def decode_attend(info, parts, own, cache, places):
    n, window, wide = cache.shape
    hd = wide // 2
    last = parts[0].shape[1] // EXTRA - 1
    return pl.pallas_call(
        decode_body,
        grid_spec=pltpu.PrefetchScalarGridSpec(
            num_scalar_prefetch=1,
            grid=(n,),
            in_specs=[
                pl.BlockSpec((p.shape[0], EXTRA, hd), lambda i, s: (0, last, 0)) for p in parts
            ]
            + [
                pl.BlockSpec((EXTRA, wide), lambda i, s: (last, 0)),
                pl.BlockSpec((1, window, wide), lambda i, s: (i, 0, 0)),
            ],
            out_specs=pl.BlockSpec((places, SLAB, 128), lambda i, s: (0, 0, 0)),
            scratch_shapes=[pltpu.VMEM((16, hd), F32), pltpu.VMEM((SLAB, 128), F32)],
        ),
        out_shape=jax.ShapeDtypeStruct((places, SLAB, 128), BF16),
        compiler_params=params(24, "arbitrary"),
        cost_estimate=pl.CostEstimate(
            flops=64 * n * hd * window, bytes_accessed=4 * n * hd * window, transcendentals=0
        ),
        name="decode_attend",
    )(info, *parts, own, cache)


def interleave_body(z_ref, *refs):
    pieces, out_ref = refs[:4], refs[4]
    run = pieces[0].shape[0] // 2
    for z in range(4):

        @pl.when(z_ref[0] == z)
        def _():
            for core in range(2):
                rows = [
                    pieces[(z - at) % 4][core * run : (core + 1) * run].astype(F32) for at in range(4)
                ]
                out_ref[core] = jnp.concatenate(rows, 0).astype(BF16)


def interleave(z, pieces):
    rows, cols = pieces[0].shape
    vmem = pl.BlockSpec(memory_space=pltpu.VMEM)
    return pl.pallas_call(
        interleave_body,
        in_specs=[pl.BlockSpec(memory_space=pltpu.SMEM)] + [vmem] * 4,
        out_specs=vmem,
        out_shape=jax.ShapeDtypeStruct((2, 2 * rows, cols), BF16),
        compiler_params=params(8),
        name="interleave",
    )(z, *pieces)


def place_body(to_ref, rows_ref, out_ref):
    for i in range(rows_ref.shape[0]):
        out_ref[to_ref[i]] = rows_ref[i]


def place(rows, to, places):
    return pl.pallas_call(
        place_body,
        in_specs=[pl.BlockSpec(memory_space=pltpu.SMEM), pl.BlockSpec(memory_space=pltpu.VMEM)],
        out_specs=pl.BlockSpec(memory_space=pltpu.VMEM),
        out_shape=jax.ShapeDtypeStruct((places,) + rows.shape[1:], BF16),
        compiler_params=params(8),
        name="place",
    )(to, rows)


def pick_body(came_ref, slab_ref, out_ref):
    out_ref[...] = slab_ref[...]


def pick(arrived, came_from):
    slab = arrived.shape[1:]
    return pl.pallas_call(
        pick_body,
        grid_spec=pltpu.PrefetchScalarGridSpec(
            num_scalar_prefetch=1,
            grid=(2,),
            in_specs=[
                pl.BlockSpec((1,) + slab, lambda i, s: (lax.shift_right_logical(s[i], 1) * 2 + i, 0, 0))
            ],
            out_specs=pl.BlockSpec((1,) + slab, lambda i, s: (i, 0, 0)),
        ),
        out_shape=jax.ShapeDtypeStruct((2,) + slab, BF16),
        compiler_params=params(8, "arbitrary"),
        name="pick",
    )(came_from, arrived)


def span_body(index_ref, ab_ref, c_ref, k_ref, v_ref, cache_ref, out_ref):
    index = index_ref[0]
    q = jnp.where(pl.program_id(0) < pl.num_programs(0) - 1, ab_ref[0], c_ref[0])
    rows, hd = q.shape
    blocks = cache_ref.shape[1] // rows
    wrapped = index >= blocks
    row = lax.broadcasted_iota(jnp.int32, (rows, rows), 0)
    col = lax.broadcasted_iota(jnp.int32, (rows, rows), 1)
    own = col <= row
    starts, scores, shifts = [], [], []
    top = None
    for rel in range(blocks):
        block = lax.rem(index + rel, blocks)
        start = pl.multiple_of(block * rows, rows)
        starts.append(start)
        s = dot_t(q, cache_ref[0, pl.ds(start, rows), :hd])
        if rel == 0:
            s = jnp.where(own, dot_t(q, k_ref[...]), jnp.where(wrapped, s, NEG))
            shift = jnp.float32(0)
        else:
            shift = jnp.where(wrapped | (block < index), jnp.float32(0), jnp.float32(NEG))
        scores.append(s)
        shifts.append(shift)
        peak = jnp.max(s, 1, keepdims=True) + shift
        top = peak if top is None else jnp.maximum(top, peak)
    scale = LOG2E * hd**-0.5
    base = top * scale
    total = jnp.zeros((rows, 1), F32)
    mixed = jnp.zeros((rows, hd), F32)
    for rel in range(blocks):
        terms = jnp.exp2(scores[rel] * scale - (base - shifts[rel]))
        total += jnp.sum(terms, 1, keepdims=True)
        old_values = cache_ref[0, pl.ds(starts[rel], rows), hd:]
        if rel == 0:
            mixed += dot(jnp.where(own, terms, 0.0).astype(BF16), v_ref[...])
            mixed += dot(jnp.where(own, 0.0, terms).astype(BF16), old_values)
        else:
            mixed += dot(terms.astype(BF16), old_values)
    out_ref[...] = (mixed / total).astype(BF16)


def span_attend(index, ab, c, key, value, rows, cache):
    heads, hd = ab.shape[0] + 1, ab.shape[2]
    window = cache.shape[1]
    return pl.pallas_call(
        span_body,
        grid_spec=pltpu.PrefetchScalarGridSpec(
            num_scalar_prefetch=1,
            grid=(heads,),
            in_specs=[
                pl.BlockSpec((1, rows, hd), lambda h, s: (jnp.minimum(h, heads - 2), 0, 0)),
                pl.BlockSpec((1, rows, hd), lambda h, s: (0, 0, 0)),
                pl.BlockSpec((rows, hd), lambda h, s: (0, 0)),
                pl.BlockSpec((rows, hd), lambda h, s: (0, 0)),
                pl.BlockSpec((1, window, 2 * hd), lambda h, s: (0, 0, 0)),
            ],
            out_specs=pl.BlockSpec((rows, hd), lambda h, s: (0, h)),
        ),
        out_shape=jax.ShapeDtypeStruct((rows, heads * hd), BF16),
        compiler_params=params(32, "arbitrary"),
        cost_estimate=pl.CostEstimate(
            flops=4 * heads * rows * hd * (window + rows),
            bytes_accessed=4 * hd * window,
            transcendentals=heads * rows * window,
        ),
        name="span_attend",
    )(index, ab, c, key, value, cache)


def finish_body(
    info_ref, att1_ref, att2_ref, datt_ref, x_ref, dx_ref, *refs
):
    chunks, (out_ref, dout_ref, lhs, w, sem) = refs[:16], refs[16:]
    rows, k = att1_ref.shape
    step = pl.program_id(0)
    core = info_ref[0]

    def copies(quarter):
        for i in range(4):
            place = info_ref[1 + quarter * 4 + i]
            if quarter % 2:
                to = w.at[quarter, place]
            else:
                to = w.at[quarter, :, :, place]
            yield pltpu.make_async_copy(chunks[quarter * 4 + i], to, sem.at[quarter, i])

    @pl.when(step == 0)
    def _():
        for quarter in range(4):
            for copy in copies(quarter):
                copy.start()
        lhs[core, :rows] = att1_ref[...]
        lhs[1 - core, :rows] = att2_ref[...]
        lhs[0, rows:] = datt_ref[:, :k]
        lhs[1, rows:] = datt_ref[:, k:]

    for quarter in range(4):

        @pl.when(step == quarter)
        def _():
            for copy in copies(quarter):
                copy.wait()

    total = None
    for half in range(2):
        right = w[step, 2 * half : 2 * half + 2].reshape(k, w.shape[-1])
        term = dot(lhs[half], right)
        total = term if total is None else total + term
    out_ref[...] = (x_ref[...].astype(F32) + total[:rows]).astype(BF16)
    dout_ref[...] = (dx_ref[...].astype(F32) + total[rows:]).astype(BF16)


def finish(info, att1, att2, datt, x, dx, chunks):
    rows, n = x.shape
    drows = dx.shape[0]
    run, bn = chunks[0].shape[2:]

    def column(i, s):
        return 0, lax.rem(s[0] * 2 + i, 4)

    return pl.pallas_call(
        finish_body,
        grid_spec=pltpu.PrefetchScalarGridSpec(
            num_scalar_prefetch=1,
            grid=(4,),
            in_specs=[
                pl.BlockSpec(att1.shape, lambda i, s: (0, 0)),
                pl.BlockSpec(att2.shape, lambda i, s: (0, 0)),
                pl.BlockSpec(datt.shape, lambda i, s: (0, 0)),
                pl.BlockSpec((rows, bn), column),
                pl.BlockSpec((drows, bn), column),
            ]
            + [pl.BlockSpec(memory_space=pl.ANY)] * 16,
            out_specs=[pl.BlockSpec((rows, bn), column), pl.BlockSpec((drows, bn), column)],
            scratch_shapes=[
                pltpu.VMEM((2, rows + drows, n // 2), BF16),
                pltpu.VMEM((4, 4, 2, 4, run, bn), BF16),
                pltpu.SemaphoreType.DMA((4, 4)),
            ],
        ),
        out_shape=[
            jax.ShapeDtypeStruct((rows, n), BF16),
            jax.ShapeDtypeStruct((drows, n), BF16),
        ],
        compiler_params=params(48, "arbitrary"),
        cost_estimate=pl.CostEstimate(
            flops=2 * rows * n * n, bytes_accessed=2 * n * n, transcendentals=0
        ),
        name="finish",
    )(info, att1, att2, datt, x, dx, *chunks)


def exchange(sent, devices):
    got = lax.all_to_all(sent.reshape((devices, -1) + sent.shape[1:]), AXES, 0, 0)
    return got.reshape(sent.shape)


STRIDE = {"y": 32, "x": 4, "z": 1}
DEVICES = np.arange(128)


def spot(axis):
    return DEVICES // STRIDE[axis] % 4


def send(v, axis, by):
    at = spot(axis)
    to = DEVICES + ((at + by) % 4 - at) * STRIDE[axis]
    return lax.ppermute(v, AXES, list(zip(DEVICES.tolist(), to.tolist())))


def swap(v):
    return lax.ppermute(v, AXES, list(zip(DEVICES.tolist(), (DEVICES ^ 16).tolist())))


RING = np.where(DEVICES // 16 % 2 == 0, 1, 3)


def put(whole, piece, index, place):
    start = [jnp.uint32(0)] * whole.ndim
    start[place] = index
    return lax.dynamic_update_slice(whole, jnp.expand_dims(piece, place), start)


def shards(
    devices,
    span_tokens,
    decode_tokens,
    norm_gain,
    query_weight,
    keyval_weight,
    output_weight,
    span_cache,
    decode_cache,
    span_index,
    decode_length,
    cache_slot,
):
    rows, width = span_tokens.shape[1:]
    own = decode_cache.shape[0]
    hd = keyval_weight.shape[1] // 2
    device = lax.axis_index(AXES).astype(jnp.uint32)
    core = ((device >> 4) & 1).astype(jnp.int32)
    first_core = core == 0
    run = query_weight.shape[0]

    half_q, half_kv = width // 2, hd
    halves = [
        jnp.concatenate(
            [
                query_weight[:, i * half_q : (i + 1) * half_q],
                keyval_weight[:, i * half_kv : (i + 1) * half_kv],
                output_weight[:, i * half_q : (i + 1) * half_q],
            ],
            1,
        )
        for i in range(2)
    ]
    got = swap(jnp.where(first_core, halves[1], halves[0]))
    piece = jnp.where(
        first_core, jnp.concatenate([halves[0], got], 0), jnp.concatenate([got, halves[1]], 0)
    )
    places = devices * own
    slots_here = (device * own).astype(jnp.int32) + jnp.arange(own, dtype=jnp.int32)
    slot_of_mine = lax.dynamic_slice(cache_slot, (device * own,), (own,))
    request_of_mine = jnp.argmax(cache_slot[None, :] == slots_here[:, None], 1).astype(jnp.int32)
    digits = jnp.stack([decode_length // 256, decode_length % 256], 1).astype(BF16)
    tagged = jnp.concatenate([decode_tokens, jnp.pad(digits, ((0, 0), (0, 510)))], 1)
    tagged = tagged.reshape(own, SLAB, 128)
    tagged = place(tagged, slot_of_mine, places)

    split = half_q + half_kv
    first_weight = lax.all_gather(piece[:, :split], CHIPS, axis=0, tiled=True)

    here = {axis: (device >> shift) & 3 for axis, shift in (("y", 5), ("x", 2), ("z", 0))}
    back = 1 - 2 * ((device >> 4) & 1)
    came = {axis: [(at - back * k) & 3 for k in range(4)] for axis, at in here.items()}
    strip, tagged = lax.optimization_barrier((piece[:, split:], tagged))
    strips = [strip] + [send(strip, "z", k) for k in (1, 2, 3)]
    strips = interleave(here["z"].astype(jnp.int32)[None], strips)
    bn = half_q // 2
    stack = [strips[:, :, :bn], strips[:, :, bn:]]
    plan = (("y", 0, "x", 2), ("x", 1, "y", 0))
    parts = [
        jnp.zeros((4, 2, 4 * run, bn), BF16),
        jnp.zeros((2, 4, 4 * run, bn), BF16),
    ]
    for k in range(4):
        for i, (axis, dim, _, _) in enumerate(plan):
            stack[i] = send(stack[i], axis, RING) if k else stack[i]
            parts[i] = put(parts[i], stack[i], came[axis][k], dim)
    arrived = pick(exchange(tagged, devices), request_of_mine)
    arrived = arrived.reshape(own, SLAB * 128)
    own_tokens = jnp.pad(arrived[:, :width], ((0, EXTRA - own), (0, 0)))
    tags = arrived[:, width : width + 2].astype(jnp.int32)
    own_length = tags[:, 0] * 256 + tags[:, 1]

    offset = span_index[0] * rows
    span_positions = offset + jnp.arange(rows, dtype=jnp.int32)
    decode_positions = jnp.pad(own_length, (0, EXTRA - own))
    positions = jnp.concatenate(
        [span_positions, swap(span_positions), decode_positions, swap(decode_positions)]
    )
    quarter = hd // 4
    frequency = 10000.0 ** (-jnp.arange(quarter, dtype=F32) / quarter)
    angles = positions.astype(F32)[:, None] * frequency
    cos, sin = jnp.cos(angles), jnp.sin(angles)
    cos = jnp.concatenate([cos, cos], 1)
    sin = jnp.concatenate([-sin, sin], 1)
    cos = jnp.stack([cos, jnp.where(first_core, cos, 1.0)])
    sin = jnp.stack([sin, jnp.where(first_core, sin, 0.0)])

    order = arrival_order(run)
    both_spans = jnp.concatenate([span_tokens[0], swap(span_tokens[0])], 0)
    both_decodes = jnp.concatenate([own_tokens, swap(own_tokens)], 0)
    total = 2 * (rows + EXTRA)
    lhs = norm_ordered(both_spans, norm_gain, order, total, 128, 0)
    at = 2 * rows // (2 * EXTRA)
    lhs = norm_ordered(both_decodes, norm_gain, order, total, 2 * EXTRA, at, (lhs,))
    mine = [[part] for part in parts]
    theirs = [[swap(part)] for part in parts]
    for k in (1, 2, 3):
        if k == 2:
            parts, lhs, cos, sin = lax.optimization_barrier((parts, lhs, cos, sin))
        parts = [send(part, p[2], RING) for part, p in zip(parts, plan)]
        for i in range(2):
            mine[i].append(parts[i])
            if k < 3:
                theirs[i].append(swap(parts[i]))
    ours_c, other_c = project(4, 2, rows, lhs, first_weight, cos, sin, hd)
    theirs_c = swap(other_c)
    ours_ab, other_ab = project(0, 4, rows, lhs, first_weight, cos, sin, hd)
    theirs_ab = swap(other_ab)
    parts, ours_ab = lax.optimization_barrier((parts, ours_ab))
    for i in range(2):
        theirs[i].append(swap(parts[i]))

    key = jnp.where(first_core, ours_c[1], theirs_c[1])
    value = jnp.where(first_core, theirs_c[1], ours_c[1])
    keyval = jnp.concatenate([key, value], 1)
    decode_keyval = keyval[rows : rows + own]
    info = jnp.concatenate([own_length, request_of_mine, core[None]])
    quarters = (ours_ab, ours_c, theirs_ab, theirs_c)
    home = exchange(decode_attend(info, quarters, keyval, decode_cache, places), devices)
    att1 = span_attend(span_index, ours_ab, ours_c, key, value, rows, span_cache)
    att2 = span_attend(span_index, theirs_ab, theirs_c, key, value, rows, span_cache)
    home = pick(home, slot_of_mine).reshape(own, SLAB * 128)[:, :width]
    shifts = jnp.asarray([2] * 4 + [5] * 4 + [2] * 4 + [5] * 4, jnp.int32)
    steps = jnp.asarray([0, 1, 2, 3] * 2 + [0, -1, -2, -3] * 2, jnp.int32)
    came_from = (((device.astype(jnp.int32) >> shifts) & 3) - (1 - 2 * core) * steps) & 3
    span_output, decode_output = finish(
        jnp.concatenate([core[None], came_from]),
        att1,
        att2,
        jnp.pad(home, ((0, EXTRA - own), (0, 0))),
        span_tokens[0],
        jnp.pad(decode_tokens, ((0, EXTRA - own), (0, 0))),
        [c for half in (mine, theirs) for part in half for c in part],
    )
    return span_output[None], keyval[:rows][None], decode_output[:own], decode_keyval


def solution(mesh):
    both = P(AXES)
    return jax.shard_map(
        functools.partial(shards, mesh.size),
        mesh=Mesh(mesh.devices.reshape(4, 2, 4, 4), AXES),
        in_specs=(both, both, P(), both, both, both, both, both, both, both, P()),
        out_specs=(both, both, both, both),
        check_vma=False,
    )
```

```python
import functools

import jax
import jax.numpy as jnp
import numpy as np
from jax import lax
from jax.experimental import pallas as pl
from jax.experimental.pallas import tpu as pltpu
from jax.sharding import Mesh
from jax.sharding import PartitionSpec as P

AXES = ("y", "c", "x", "z")
CHIPS = ("y", "x", "z")
LOG2E = 1.4426950408889634
NEG = -1e30
F32 = jnp.float32
BF16 = jnp.bfloat16
EXTRA = 16


def params(mib, *semantics):
    return pltpu.CompilerParams(vmem_limit_bytes=mib << 20, dimension_semantics=semantics or None)


def dot(a, b):
    return jnp.dot(a, b, preferred_element_type=F32)


def dot_t(a, b):
    return lax.dot_general(a, b, (((1,), (1,)), ((), ())), preferred_element_type=F32)


def mover(to, width):
    return (jnp.asarray(to, jnp.int32)[:, None] == jnp.arange(width)[None, :]).astype(BF16)


def arrival_order(run):
    core, x, z, r = np.meshgrid(*(np.arange(n) for n in (2, 4, 4, run)), indexing="ij")
    return mover((((x * 4 + z) * 2 + core) * run + r).reshape(-1), 32 * run)


def norm_body(x_ref, gain_ref, order_ref, *refs):
    out_ref = refs[-1]
    x = x_ref[...].astype(F32)
    rows = x.shape[0]
    mean = jnp.mean(x * x, axis=-1, keepdims=True)
    normed = (x * lax.rsqrt(mean + 1e-06) * gain_ref[...]).astype(BF16)
    k = order_ref.shape[0]
    blocks = jnp.concatenate([normed[:, y * k : (y + 1) * k] for y in range(4)], 0)
    moved = dot(blocks, order_ref[...]).astype(BF16)
    for y in range(4):
        out_ref[:, y * k : (y + 1) * k] = moved[y * rows : (y + 1) * rows]


def norm_ordered(x, gain, order, total, block, at, into=()):
    rows, width = x.shape
    return pl.pallas_call(
        norm_body,
        grid=(rows // block,),
        in_specs=[
            pl.BlockSpec((block, width), lambda i: (i, 0)),
            pl.BlockSpec((1, width), lambda i: (0, 0)),
            pl.BlockSpec(order.shape, lambda i: (0, 0)),
        ]
        + [pl.BlockSpec(memory_space=pl.ANY)] * len(into),
        out_specs=pl.BlockSpec((block, width), lambda i: (at + i, 0)),
        out_shape=jax.ShapeDtypeStruct((total, width), BF16),
        input_output_aliases={3 + i: i for i in range(len(into))},
        compiler_params=params(24, "arbitrary"),
        cost_estimate=pl.CostEstimate(
            flops=2 * rows * width * 640, bytes_accessed=4 * rows * width, transcendentals=0
        ),
        name="norm_ordered",
    )(x, gain[None], order, *into)


def rotate(v, cos_ref, sin_ref):
    half = v[:, :128]
    turned = half * cos_ref[...] + pltpu.roll(half, 64, 1) * sin_ref[...]
    return jnp.concatenate([turned, v[:, 128:]], 1)


def project_body(rows, x_ref, w_ref, cos_ref, sin_ref, ours_ref, other_ref):
    extra = ours_ref.shape[1] - rows
    made = rotate(dot(x_ref[...], w_ref[...]), cos_ref.at[0], sin_ref.at[0]).astype(BF16)
    ours_ref[0, :rows] = made[:rows]
    other_ref[0, :rows] = made[rows : 2 * rows]
    ours_ref[0, rows:] = made[2 * rows : 2 * rows + extra]
    other_ref[0, rows:] = made[2 * rows + extra :]


def project(first, count, rows, x, w, cos, sin, hd):
    total, depth = x.shape
    last = w.shape[1] // hd - 1
    shape = jax.ShapeDtypeStruct((count, total // 2, hd), BF16)
    table = pl.BlockSpec((1, total, 128), lambda i: ((first + i) // last, 0, 0))
    return pl.pallas_call(
        functools.partial(project_body, rows),
        grid=(count,),
        in_specs=[
            pl.BlockSpec((total, depth), lambda i: (0, 0)),
            pl.BlockSpec((depth, hd), lambda i: (0, first + i)),
            table,
            table,
        ],
        out_specs=[pl.BlockSpec((1, total // 2, hd), lambda i: (i, 0, 0))] * 2,
        out_shape=[shape, shape],
        compiler_params=params(32, "arbitrary"),
        cost_estimate=pl.CostEstimate(
            flops=2 * total * count * depth * hd,
            bytes_accessed=2 * count * depth * hd,
            transcendentals=0,
        ),
        name="project",
    )(x, w, cos, sin)


SLAB = 24


def decode_body(
    info_ref, oab_ref, oc_ref, tab_ref, tc_ref, own_ref, cache_ref, out_ref, gather_ref, spill_ref
):
    i = pl.program_id(0)
    length, to, core = info_ref[i], info_ref[2 + i], info_ref[4]
    hd = cache_ref.shape[2] // 2
    window = cache_ref.shape[1]
    for half, (ab_ref, c_ref) in enumerate(((oab_ref, oc_ref), (tab_ref, tc_ref))):
        for h in range(5):
            block = ab_ref[h] if h < 4 else c_ref[0]
            block = block.astype(F32)
            row = jnp.where(i == 0, block[0:1], block[1:2])
            gather_ref[half * 5 + h : half * 5 + h + 1] = row
    gather_ref[10:16] = jnp.zeros((6, hd), F32)
    q = gather_ref[...].astype(BF16)
    scores = dot_t(q, cache_ref[0, :, :hd])
    own_row = own_ref[...].astype(F32)
    own_row = jnp.where(i == 0, own_row[0:1], own_row[1:2])
    own = jnp.sum(gather_ref[...] * own_row[:, :hd], axis=1, keepdims=True)
    slot = lax.broadcasted_iota(jnp.int32, scores.shape, 1)
    met = (slot < length) & (slot != lax.rem(length, window))
    scores = jnp.where(met, scores, NEG)
    top = jnp.maximum(jnp.max(scores, 1, keepdims=True), own)
    scale = LOG2E * hd**-0.5
    terms = jnp.where(met, jnp.exp2((scores - top) * scale), 0.0)
    own_term = jnp.exp2((own - top) * scale)
    total = jnp.sum(terms, 1, keepdims=True) + own_term
    weights = (terms / total).astype(BF16)
    own_weight = (own_term / total).astype(BF16).astype(F32)
    mixed = dot(weights, cache_ref[0, :, hd:]) + own_weight * own_row[:, hd:]
    spill_ref[20:] = jnp.zeros((SLAB - 20, 128), F32)
    for h in range(10):
        head = jnp.where(core == 0, h, (h + 5) % 10)
        for part in range(2):
            spill_ref[pl.ds(2 * head + part, 1)] = mixed[h : h + 1, part * 128 : part * 128 + 128]
    out_ref[to] = spill_ref[...].astype(BF16)


def decode_attend(info, parts, own, cache, places):
    n, window, wide = cache.shape
    hd = wide // 2
    last = parts[0].shape[1] // EXTRA - 1
    return pl.pallas_call(
        decode_body,
        grid_spec=pltpu.PrefetchScalarGridSpec(
            num_scalar_prefetch=1,
            grid=(n,),
            in_specs=[
                pl.BlockSpec((p.shape[0], EXTRA, hd), lambda i, s: (0, last, 0)) for p in parts
            ]
            + [
                pl.BlockSpec((EXTRA, wide), lambda i, s: (last, 0)),
                pl.BlockSpec((1, window, wide), lambda i, s: (i, 0, 0)),
            ],
            out_specs=pl.BlockSpec((places, SLAB, 128), lambda i, s: (0, 0, 0)),
            scratch_shapes=[pltpu.VMEM((16, hd), F32), pltpu.VMEM((SLAB, 128), F32)],
        ),
        out_shape=jax.ShapeDtypeStruct((places, SLAB, 128), BF16),
        compiler_params=params(24, "arbitrary"),
        cost_estimate=pl.CostEstimate(
            flops=64 * n * hd * window, bytes_accessed=4 * n * hd * window, transcendentals=0
        ),
        name="decode_attend",
    )(info, *parts, own, cache)


def interleave_body(z_ref, *refs):
    pieces, out_ref = refs[:4], refs[4]
    run = pieces[0].shape[0] // 2
    for z in range(4):

        @pl.when(z_ref[0] == z)
        def _():
            for core in range(2):
                rows = [
                    pieces[(z - at) % 4][core * run : (core + 1) * run].astype(F32) for at in range(4)
                ]
                out_ref[core] = jnp.concatenate(rows, 0).astype(BF16)


def interleave(z, pieces):
    rows, cols = pieces[0].shape
    vmem = pl.BlockSpec(memory_space=pltpu.VMEM)
    return pl.pallas_call(
        interleave_body,
        in_specs=[pl.BlockSpec(memory_space=pltpu.SMEM)] + [vmem] * 4,
        out_specs=vmem,
        out_shape=jax.ShapeDtypeStruct((2, 2 * rows, cols), BF16),
        compiler_params=params(8),
        name="interleave",
    )(z, *pieces)


def place_body(slot_ref, here_ref, rows_ref, out_ref):
    here = here_ref[0]
    for i in range(rows_ref.shape[0]):
        core, z, each = i // 8, i // 2 % 4, i % 2
        source = (here & 0b1101100) | (core * 16 + z)
        slot = slot_ref[source * 2 + each]
        to = slot >> 1

        @pl.when((to & 0b0010011) == (here & 0b0010011))
        def _():
            chip = ((to >> 5) << 2) | ((to >> 2) & 3)
            out_ref[chip * 2 + (slot & 1)] = rows_ref[i]


def place(slots, here, rows):
    smem = pl.BlockSpec(memory_space=pltpu.SMEM)
    vmem = pl.BlockSpec(memory_space=pltpu.VMEM)
    return pl.pallas_call(
        place_body,
        in_specs=[smem, smem, vmem],
        out_specs=vmem,
        out_shape=jax.ShapeDtypeStruct((32,) + rows.shape[1:], BF16),
        compiler_params=params(8),
        name="place",
    )(slots, here, rows)


def pick_body(came_ref, slab_ref, out_ref):
    out_ref[...] = slab_ref[...]


def by_device(came):
    return came >> 1


def by_chip(came):
    return ((came >> 6) << 2) | ((came >> 3) & 3)


def pick(arrived, came_from, where):
    slab = arrived.shape[1:]
    return pl.pallas_call(
        pick_body,
        grid_spec=pltpu.PrefetchScalarGridSpec(
            num_scalar_prefetch=1,
            grid=(2,),
            in_specs=[
                pl.BlockSpec((1,) + slab, lambda i, s: (where(s[i]) * 2 + i, 0, 0))
            ],
            out_specs=pl.BlockSpec((1,) + slab, lambda i, s: (i, 0, 0)),
        ),
        out_shape=jax.ShapeDtypeStruct((2,) + slab, BF16),
        compiler_params=params(8, "arbitrary"),
        name="pick",
    )(came_from, arrived)


def span_body(index_ref, ab1_ref, c1_ref, ab2_ref, c2_ref, k_ref, v_ref, cache_ref, out_ref):
    index = index_ref[0]
    last = pl.program_id(0) == pl.num_programs(0) - 1
    rows, hd = k_ref.shape
    q = jnp.concatenate(
        [jnp.where(last, c1_ref[0], ab1_ref[0]), jnp.where(last, c2_ref[0], ab2_ref[0])], 0
    )
    both = 2 * rows
    blocks = cache_ref.shape[1] // rows
    wrapped = index >= blocks
    row = lax.rem(lax.broadcasted_iota(jnp.int32, (both, rows), 0), rows)
    col = lax.broadcasted_iota(jnp.int32, (both, rows), 1)
    own = col <= row
    starts, scores, shifts = [], [], []
    top = None
    for rel in range(blocks):
        block = lax.rem(index + rel, blocks)
        start = pl.multiple_of(block * rows, rows)
        starts.append(start)
        s = dot_t(q, cache_ref[0, pl.ds(start, rows), :hd])
        if rel == 0:
            s = jnp.where(own, dot_t(q, k_ref[...]), jnp.where(wrapped, s, NEG))
            shift = jnp.float32(0)
        else:
            shift = jnp.where(wrapped | (block < index), jnp.float32(0), jnp.float32(NEG))
        scores.append(s)
        shifts.append(shift)
        peak = jnp.max(s, 1, keepdims=True) + shift
        top = peak if top is None else jnp.maximum(top, peak)
    scale = LOG2E * hd**-0.5
    base = top * scale
    total = jnp.zeros((both, 1), F32)
    mixed = jnp.zeros((both, hd), F32)
    for rel in range(blocks):
        terms = jnp.exp2(scores[rel] * scale - (base - shifts[rel]))
        total += jnp.sum(terms, 1, keepdims=True)
        old_values = cache_ref[0, pl.ds(starts[rel], rows), hd:]
        if rel == 0:
            mixed += dot(jnp.where(own, terms, 0.0).astype(BF16), v_ref[...])
            mixed += dot(jnp.where(own, 0.0, terms).astype(BF16), old_values)
        else:
            mixed += dot(terms.astype(BF16), old_values)
    made = (mixed / total).astype(BF16)
    out_ref[0] = made[:rows]
    out_ref[1] = made[rows:]


def span_attend(index, ours, theirs, key, value, rows, cache):
    half, hd = ours[0].shape[0] + 1, ours[0].shape[2]
    heads = 2 * half
    window = cache.shape[1]
    many = pl.BlockSpec((1, rows, hd), lambda h, s: (jnp.minimum(h, half - 2), 0, 0))
    single = pl.BlockSpec((1, rows, hd), lambda h, s: (0, 0, 0))
    pair = pl.BlockSpec((rows, hd), lambda h, s: (0, 0))
    return pl.pallas_call(
        span_body,
        grid_spec=pltpu.PrefetchScalarGridSpec(
            num_scalar_prefetch=1,
            grid=(half,),
            in_specs=[many, single, many, single, pair, pair]
            + [pl.BlockSpec((1, window, 2 * hd), lambda h, s: (0, 0, 0))],
            out_specs=pl.BlockSpec((2, rows, hd), lambda h, s: (0, 0, h)),
        ),
        out_shape=jax.ShapeDtypeStruct((2, rows, half * hd), BF16),
        compiler_params=params(36, "arbitrary"),
        cost_estimate=pl.CostEstimate(
            flops=4 * heads * rows * hd * (window + rows),
            bytes_accessed=4 * hd * window,
            transcendentals=heads * rows * window,
        ),
        name="span_attend",
    )(index, *ours, *theirs, key, value, cache)


def finish_body(
    info_ref, att_ref, datt_ref, x_ref, dx_ref, *refs
):
    chunks, (out_ref, dout_ref, lhs, w, sem) = refs[:16], refs[16:]
    rows, k = att_ref.shape[1:]
    step = pl.program_id(0)
    core = info_ref[0]

    def copies(quarter):
        for i in range(4):
            place = info_ref[1 + quarter * 4 + i]
            if quarter % 2:
                to = w.at[quarter, place]
            else:
                to = w.at[quarter, :, :, place]
            yield pltpu.make_async_copy(chunks[quarter * 4 + i], to, sem.at[quarter, i])

    @pl.when(step == 0)
    def _():
        for quarter in range(4):
            for copy in copies(quarter):
                copy.start()
        lhs[core, :rows] = att_ref[0]
        lhs[1 - core, :rows] = att_ref[1]
        lhs[0, rows:] = datt_ref[:, :k]
        lhs[1, rows:] = datt_ref[:, k:]

    for quarter in range(4):

        @pl.when(step == quarter)
        def _():
            for copy in copies(quarter):
                copy.wait()

    total = None
    for half in range(2):
        right = w[step, 2 * half : 2 * half + 2].reshape(k, w.shape[-1])
        term = dot(lhs[half], right)
        total = term if total is None else total + term
    out_ref[...] = (x_ref[...].astype(F32) + total[:rows]).astype(BF16)
    dout_ref[...] = (dx_ref[...].astype(F32) + total[rows:]).astype(BF16)


def finish(info, att, datt, x, dx, chunks):
    rows, n = x.shape
    drows = dx.shape[0]
    run, bn = chunks[0].shape[2:]

    def column(i, s):
        return 0, lax.rem(s[0] * 2 + i, 4)

    return pl.pallas_call(
        finish_body,
        grid_spec=pltpu.PrefetchScalarGridSpec(
            num_scalar_prefetch=1,
            grid=(4,),
            in_specs=[
                pl.BlockSpec(att.shape, lambda i, s: (0, 0, 0)),
                pl.BlockSpec(datt.shape, lambda i, s: (0, 0)),
                pl.BlockSpec((rows, bn), column),
                pl.BlockSpec((drows, bn), column),
            ]
            + [pl.BlockSpec(memory_space=pl.ANY)] * 16,
            out_specs=[pl.BlockSpec((rows, bn), column), pl.BlockSpec((drows, bn), column)],
            scratch_shapes=[
                pltpu.VMEM((2, rows + drows, n // 2), BF16),
                pltpu.VMEM((4, 4, 2, 4, run, bn), BF16),
                pltpu.SemaphoreType.DMA((4, 4)),
            ],
        ),
        out_shape=[
            jax.ShapeDtypeStruct((rows, n), BF16),
            jax.ShapeDtypeStruct((drows, n), BF16),
        ],
        compiler_params=params(60, "arbitrary"),
        cost_estimate=pl.CostEstimate(
            flops=2 * rows * n * n, bytes_accessed=2 * n * n, transcendentals=0
        ),
        name="finish",
    )(info, att, datt, x, dx, *chunks)


def exchange(sent, axes):
    members = lax.axis_size(axes)
    got = lax.all_to_all(sent.reshape((members, -1) + sent.shape[1:]), axes, 0, 0)
    return got.reshape(sent.shape)


STRIDE = {"y": 32, "x": 4, "z": 1}
DEVICES = np.arange(128)


def spot(axis):
    return DEVICES // STRIDE[axis] % 4


def send(v, axis, by):
    at = spot(axis)
    to = DEVICES + ((at + by) % 4 - at) * STRIDE[axis]
    return lax.ppermute(v, AXES, list(zip(DEVICES.tolist(), to.tolist())))


def swap(v):
    return lax.ppermute(v, AXES, list(zip(DEVICES.tolist(), (DEVICES ^ 16).tolist())))


RING = np.where(DEVICES // 16 % 2 == 0, 1, 3)


def put(whole, piece, index, place):
    start = [jnp.uint32(0)] * whole.ndim
    start[place] = index
    return lax.dynamic_update_slice(whole, jnp.expand_dims(piece, place), start)


def shards(
    devices,
    span_tokens,
    decode_tokens,
    norm_gain,
    query_weight,
    keyval_weight,
    output_weight,
    span_cache,
    decode_cache,
    span_index,
    decode_length,
    cache_slot,
):
    rows, width = span_tokens.shape[1:]
    own = decode_cache.shape[0]
    hd = keyval_weight.shape[1] // 2
    device = lax.axis_index(AXES).astype(jnp.uint32)
    core = ((device >> 4) & 1).astype(jnp.int32)
    first_core = core == 0
    run = query_weight.shape[0]

    half_q, half_kv = width // 2, hd
    halves = [
        jnp.concatenate(
            [
                query_weight[:, i * half_q : (i + 1) * half_q],
                keyval_weight[:, i * half_kv : (i + 1) * half_kv],
                output_weight[:, i * half_q : (i + 1) * half_q],
            ],
            1,
        )
        for i in range(2)
    ]
    got = swap(jnp.where(first_core, halves[1], halves[0]))
    piece = jnp.where(
        first_core, jnp.concatenate([halves[0], got], 0), jnp.concatenate([got, halves[1]], 0)
    )
    places = devices * own
    slots_here = (device * own).astype(jnp.int32) + jnp.arange(own, dtype=jnp.int32)
    slot_of_mine = lax.dynamic_slice(cache_slot, (device * own,), (own,))
    request_of_mine = jnp.argmax(cache_slot[None, :] == slots_here[:, None], 1).astype(jnp.int32)
    digits = jnp.stack([decode_length // 256, decode_length % 256], 1).astype(BF16)
    tagged = jnp.concatenate([decode_tokens, jnp.pad(digits, ((0, 0), (0, 510)))], 1)
    tagged = tagged.reshape(own, SLAB, 128)
    tagged = jnp.broadcast_to(tagged, (8,) + tagged.shape).reshape(8 * own, SLAB, 128)
    split = half_q + half_kv
    first_weight = lax.all_gather(piece[:, :split], CHIPS, axis=0, tiled=True)

    here = {axis: (device >> shift) & 3 for axis, shift in (("y", 5), ("x", 2), ("z", 0))}
    back = 1 - 2 * ((device >> 4) & 1)
    came = {axis: [(at - back * k) & 3 for k in range(4)] for axis, at in here.items()}
    strip = piece[:, split:]
    strips = [strip] + [send(strip, "z", k) for k in (1, 2, 3)]
    tagged, _ = lax.optimization_barrier((tagged, strips))
    tagged = place(cache_slot, device.astype(jnp.int32)[None], exchange(tagged, ("c", "z")))
    strips = interleave(here["z"].astype(jnp.int32)[None], strips)
    bn = half_q // 2
    stack = [strips[:, :, :bn], strips[:, :, bn:]]
    plan = (("y", 0, "x", 2), ("x", 1, "y", 0))
    parts = [
        jnp.zeros((4, 2, 4 * run, bn), BF16),
        jnp.zeros((2, 4, 4 * run, bn), BF16),
    ]
    for k in range(4):
        for i, (axis, dim, _, _) in enumerate(plan):
            stack[i] = send(stack[i], axis, RING) if k else stack[i]
            parts[i] = put(parts[i], stack[i], came[axis][k], dim)
    arrived = pick(exchange(tagged, ("y", "x")), request_of_mine, by_chip)
    arrived = arrived.reshape(own, SLAB * 128)
    own_tokens = jnp.pad(arrived[:, :width], ((0, EXTRA - own), (0, 0)))
    tags = arrived[:, width : width + 2].astype(jnp.int32)
    own_length = tags[:, 0] * 256 + tags[:, 1]

    offset = span_index[0] * rows
    span_positions = offset + jnp.arange(rows, dtype=jnp.int32)
    decode_positions = jnp.pad(own_length, (0, EXTRA - own))
    positions = jnp.concatenate(
        [span_positions, swap(span_positions), decode_positions, swap(decode_positions)]
    )
    quarter = hd // 4
    frequency = 10000.0 ** (-jnp.arange(quarter, dtype=F32) / quarter)
    angles = positions.astype(F32)[:, None] * frequency
    cos, sin = jnp.cos(angles), jnp.sin(angles)
    cos = jnp.concatenate([cos, cos], 1)
    sin = jnp.concatenate([-sin, sin], 1)
    cos = jnp.stack([cos, jnp.where(first_core, cos, 1.0)])
    sin = jnp.stack([sin, jnp.where(first_core, sin, 0.0)])

    order = arrival_order(run)
    both_spans = jnp.concatenate([span_tokens[0], swap(span_tokens[0])], 0)
    both_decodes = jnp.concatenate([own_tokens, swap(own_tokens)], 0)
    total = 2 * (rows + EXTRA)
    lhs = norm_ordered(both_spans, norm_gain, order, total, 128, 0)
    at = 2 * rows // (2 * EXTRA)
    lhs = norm_ordered(both_decodes, norm_gain, order, total, 2 * EXTRA, at, (lhs,))
    mine = [[part] for part in parts]
    theirs = [[swap(part)] for part in parts]
    def ring_step(parts):
        parts = [send(part, p[2], RING) for part, p in zip(parts, plan)]
        for i in range(2):
            mine[i].append(parts[i])
        return parts

    def swap_last(after):
        parts, _ = lax.optimization_barrier(([m[-1] for m in mine], after))
        for i in range(2):
            theirs[i].append(swap(parts[i]))

    parts = ring_step(parts)
    swap_last(())
    shifts = jnp.asarray([2] * 4 + [5] * 4 + [2] * 4 + [5] * 4, jnp.int32)
    steps = jnp.asarray([0, 1, 2, 3] * 2 + [0, -1, -2, -3] * 2, jnp.int32)
    came_from = (((device.astype(jnp.int32) >> shifts) & 3) - (1 - 2 * core) * steps) & 3
    finish_info = jnp.concatenate([core[None], came_from])
    decode_rows = jnp.pad(decode_tokens, ((0, EXTRA - own), (0, 0)))
    info = jnp.concatenate([own_length, request_of_mine, core[None]])
    parts, lhs, cos, sin, finish_info, decode_rows, info = lax.optimization_barrier(
        (parts, lhs, cos, sin, finish_info, decode_rows, info)
    )
    ring_step(parts)
    first_weight = pltpu.with_memory_space_constraint(first_weight, pltpu.HBM)
    ours_c, other_c = project(4, 2, rows, lhs, first_weight, cos, sin, hd)
    theirs_c = swap(other_c)
    ours_ab, other_ab = project(0, 4, rows, lhs, first_weight, cos, sin, hd)
    theirs_ab = swap(other_ab)
    swap_last(ours_ab)
    parts, _ = lax.optimization_barrier(([m[-1] for m in mine], ours_ab))
    ring_step(parts)

    key = jnp.where(first_core, ours_c[1], theirs_c[1])
    value = jnp.where(first_core, theirs_c[1], ours_c[1])
    keyval = jnp.concatenate([key, value], 1)
    decode_keyval = keyval[rows : rows + own]
    quarters = (ours_ab, ours_c, theirs_ab, theirs_c)
    routed = decode_attend(info, quarters, keyval, decode_cache, places)
    home = exchange(routed, AXES)
    swap_last(routed)
    att = span_attend(
        span_index, (ours_ab, ours_c), (theirs_ab, theirs_c), key, value, rows, span_cache
    )
    home = pick(home, slot_of_mine, by_device).reshape(own, SLAB * 128)[:, :width]
    span_output, decode_output = finish(
        finish_info,
        att,
        jnp.pad(home, ((0, EXTRA - own), (0, 0))),
        span_tokens[0],
        decode_rows,
        [c for half in (mine, theirs) for part in half for c in part],
    )
    return span_output[None], keyval[:rows][None], decode_output[:own], decode_keyval


def solution(mesh):
    both = P(AXES)
    return jax.shard_map(
        functools.partial(shards, mesh.size),
        mesh=Mesh(mesh.devices.reshape(4, 2, 4, 4), AXES),
        in_specs=(both, both, P(), both, both, both, both, both, both, both, P()),
        out_specs=(both, both, both, both),
        check_vma=False,
    )
```

```python
import functools

import jax
import jax.numpy as jnp
import numpy as np
from jax import lax
from jax.experimental import pallas as pl
from jax.experimental.pallas import tpu as pltpu
from jax.sharding import Mesh
from jax.sharding import PartitionSpec as P

AXES = ("y", "c", "x", "z")
CHIPS = ("y", "x", "z")
LOG2E = 1.4426950408889634
NEG = -1e30
F32 = jnp.float32
BF16 = jnp.bfloat16
EXTRA = 16


def params(mib, *semantics):
    return pltpu.CompilerParams(vmem_limit_bytes=mib << 20, dimension_semantics=semantics or None)


def dot(a, b):
    return jnp.dot(a, b, preferred_element_type=F32)


def dot_t(a, b):
    return lax.dot_general(a, b, (((1,), (1,)), ((), ())), preferred_element_type=F32)


def mover(to, width):
    return (jnp.asarray(to, jnp.int32)[:, None] == jnp.arange(width)[None, :]).astype(BF16)


def arrival_order(run):
    core, x, z, r = np.meshgrid(*(np.arange(n) for n in (2, 4, 4, run)), indexing="ij")
    return mover((((x * 4 + z) * 2 + core) * run + r).reshape(-1), 32 * run)


def norm_body(x_ref, gain_ref, order_ref, *refs):
    out_ref = refs[-1]
    x = x_ref[...].astype(F32)
    rows = x.shape[0]
    mean = jnp.mean(x * x, axis=-1, keepdims=True)
    normed = (x * lax.rsqrt(mean + 1e-06) * gain_ref[...]).astype(BF16)
    k = order_ref.shape[0]
    blocks = jnp.concatenate([normed[:, y * k : (y + 1) * k] for y in range(4)], 0)
    moved = dot(blocks, order_ref[...]).astype(BF16)
    for y in range(4):
        out_ref[:, y * k : (y + 1) * k] = moved[y * rows : (y + 1) * rows]


def norm_ordered(x, gain, order, total, block, at, into=()):
    rows, width = x.shape
    return pl.pallas_call(
        norm_body,
        grid=(rows // block,),
        in_specs=[
            pl.BlockSpec((block, width), lambda i: (i, 0)),
            pl.BlockSpec((1, width), lambda i: (0, 0)),
            pl.BlockSpec(order.shape, lambda i: (0, 0)),
        ]
        + [pl.BlockSpec(memory_space=pl.ANY)] * len(into),
        out_specs=pl.BlockSpec((block, width), lambda i: (at + i, 0)),
        out_shape=jax.ShapeDtypeStruct((total, width), BF16),
        input_output_aliases={3 + i: i for i in range(len(into))},
        compiler_params=params(24, "arbitrary"),
        cost_estimate=pl.CostEstimate(
            flops=2 * rows * width * 640, bytes_accessed=4 * rows * width, transcendentals=0
        ),
        name="norm_ordered",
    )(x, gain[None], order, *into)


def rotate(v, cos_ref, sin_ref):
    half = v[:, :128]
    turned = half * cos_ref[...] + pltpu.roll(half, 64, 1) * sin_ref[...]
    return jnp.concatenate([turned, v[:, 128:]], 1)


def project_body(rows, x_ref, w_ref, cos_ref, sin_ref, ours_ref, other_ref):
    extra = ours_ref.shape[1] - rows
    made = rotate(dot(x_ref[...], w_ref[...]), cos_ref.at[0], sin_ref.at[0]).astype(BF16)
    ours_ref[0, :rows] = made[:rows]
    other_ref[0, :rows] = made[rows : 2 * rows]
    ours_ref[0, rows:] = made[2 * rows : 2 * rows + extra]
    other_ref[0, rows:] = made[2 * rows + extra :]


def project(first, count, rows, x, w, cos, sin, hd):
    total, depth = x.shape
    last = w.shape[1] // hd - 1
    shape = jax.ShapeDtypeStruct((count, total // 2, hd), BF16)
    table = pl.BlockSpec((1, total, 128), lambda i: ((first + i) // last, 0, 0))
    return pl.pallas_call(
        functools.partial(project_body, rows),
        grid=(count,),
        in_specs=[
            pl.BlockSpec((total, depth), lambda i: (0, 0)),
            pl.BlockSpec((depth, hd), lambda i: (0, first + i)),
            table,
            table,
        ],
        out_specs=[pl.BlockSpec((1, total // 2, hd), lambda i: (i, 0, 0))] * 2,
        out_shape=[shape, shape],
        compiler_params=params(32, "arbitrary"),
        cost_estimate=pl.CostEstimate(
            flops=2 * total * count * depth * hd,
            bytes_accessed=2 * count * depth * hd,
            transcendentals=0,
        ),
        name="project",
    )(x, w, cos, sin)


SLAB = 24


def decode_body(
    info_ref, oab_ref, oc_ref, tab_ref, tc_ref, own_ref, cache_ref, out_ref, gather_ref, spill_ref
):
    i = pl.program_id(0)
    length, to, core = info_ref[i], info_ref[2 + i], info_ref[4]
    hd = cache_ref.shape[2] // 2
    window = cache_ref.shape[1]
    for half, (ab_ref, c_ref) in enumerate(((oab_ref, oc_ref), (tab_ref, tc_ref))):
        for h in range(5):
            block = ab_ref[h] if h < 4 else c_ref[0]
            block = block.astype(F32)
            row = jnp.where(i == 0, block[0:1], block[1:2])
            gather_ref[half * 5 + h : half * 5 + h + 1] = row
    gather_ref[10:16] = jnp.zeros((6, hd), F32)
    q = gather_ref[...].astype(BF16)
    scores = dot_t(q, cache_ref[0, :, :hd])
    own_row = own_ref[...].astype(F32)
    own_row = jnp.where(i == 0, own_row[0:1], own_row[1:2])
    own = jnp.sum(gather_ref[...] * own_row[:, :hd], axis=1, keepdims=True)
    slot = lax.broadcasted_iota(jnp.int32, scores.shape, 1)
    met = (slot < length) & (slot != lax.rem(length, window))
    scores = jnp.where(met, scores, NEG)
    top = jnp.maximum(jnp.max(scores, 1, keepdims=True), own)
    scale = LOG2E * hd**-0.5
    terms = jnp.where(met, jnp.exp2((scores - top) * scale), 0.0)
    own_term = jnp.exp2((own - top) * scale)
    total = jnp.sum(terms, 1, keepdims=True) + own_term
    weights = (terms / total).astype(BF16)
    own_weight = (own_term / total).astype(BF16).astype(F32)
    mixed = dot(weights, cache_ref[0, :, hd:]) + own_weight * own_row[:, hd:]
    spill_ref[20:] = jnp.zeros((SLAB - 20, 128), F32)
    for h in range(10):
        head = jnp.where(core == 0, h, (h + 5) % 10)
        for part in range(2):
            spill_ref[pl.ds(2 * head + part, 1)] = mixed[h : h + 1, part * 128 : part * 128 + 128]
    out_ref[to] = spill_ref[...].astype(BF16)


def decode_attend(info, parts, own, cache, places):
    n, window, wide = cache.shape
    hd = wide // 2
    last = parts[0].shape[1] // EXTRA - 1
    return pl.pallas_call(
        decode_body,
        grid_spec=pltpu.PrefetchScalarGridSpec(
            num_scalar_prefetch=1,
            grid=(n,),
            in_specs=[
                pl.BlockSpec((p.shape[0], EXTRA, hd), lambda i, s: (0, last, 0)) for p in parts
            ]
            + [
                pl.BlockSpec((EXTRA, wide), lambda i, s: (last, 0)),
                pl.BlockSpec((1, window, wide), lambda i, s: (i, 0, 0)),
            ],
            out_specs=pl.BlockSpec((places, SLAB, 128), lambda i, s: (0, 0, 0)),
            scratch_shapes=[pltpu.VMEM((16, hd), F32), pltpu.VMEM((SLAB, 128), F32)],
        ),
        out_shape=jax.ShapeDtypeStruct((places, SLAB, 128), BF16),
        compiler_params=params(24, "arbitrary"),
        cost_estimate=pl.CostEstimate(
            flops=64 * n * hd * window, bytes_accessed=4 * n * hd * window, transcendentals=0
        ),
        name="decode_attend",
    )(info, *parts, own, cache)


def interleave_body(z_ref, *refs):
    pieces, out_ref = refs[:4], refs[4]
    run = pieces[0].shape[0] // 2
    for z in range(4):

        @pl.when(z_ref[0] == z)
        def _():
            for core in range(2):
                rows = [
                    pieces[(z - at) % 4][core * run : (core + 1) * run].astype(F32) for at in range(4)
                ]
                out_ref[core] = jnp.concatenate(rows, 0).astype(BF16)


def interleave(z, pieces):
    rows, cols = pieces[0].shape
    vmem = pl.BlockSpec(memory_space=pltpu.VMEM)
    return pl.pallas_call(
        interleave_body,
        in_specs=[pl.BlockSpec(memory_space=pltpu.SMEM)] + [vmem] * 4,
        out_specs=vmem,
        out_shape=jax.ShapeDtypeStruct((2, 2 * rows, cols), BF16),
        compiler_params=params(8),
        name="interleave",
    )(z, *pieces)


def place_body(slot_ref, here_ref, rows_ref, out_ref):
    here = here_ref[0]
    for i in range(rows_ref.shape[0]):
        core, z, each = i // 8, i // 2 % 4, i % 2
        source = (here & 0b1101100) | (core * 16 + z)
        slot = slot_ref[source * 2 + each]
        to = slot >> 1

        @pl.when((to & 0b0010011) == (here & 0b0010011))
        def _():
            chip = ((to >> 5) << 2) | ((to >> 2) & 3)
            out_ref[chip * 2 + (slot & 1)] = rows_ref[i]


def place(slots, here, rows):
    smem = pl.BlockSpec(memory_space=pltpu.SMEM)
    vmem = pl.BlockSpec(memory_space=pltpu.VMEM)
    return pl.pallas_call(
        place_body,
        in_specs=[smem, smem, vmem],
        out_specs=vmem,
        out_shape=jax.ShapeDtypeStruct((32,) + rows.shape[1:], BF16),
        compiler_params=params(8),
        name="place",
    )(slots, here, rows)


def pick_body(came_ref, slab_ref, out_ref):
    out_ref[...] = slab_ref[...]


def by_device(came):
    return came >> 1


def by_chip(came):
    return ((came >> 6) << 2) | ((came >> 3) & 3)


def pick(arrived, came_from, where):
    slab = arrived.shape[1:]
    return pl.pallas_call(
        pick_body,
        grid_spec=pltpu.PrefetchScalarGridSpec(
            num_scalar_prefetch=1,
            grid=(2,),
            in_specs=[
                pl.BlockSpec((1,) + slab, lambda i, s: (where(s[i]) * 2 + i, 0, 0))
            ],
            out_specs=pl.BlockSpec((1,) + slab, lambda i, s: (i, 0, 0)),
        ),
        out_shape=jax.ShapeDtypeStruct((2,) + slab, BF16),
        compiler_params=params(8, "arbitrary"),
        name="pick",
    )(came_from, arrived)


def span_body(index_ref, ab1_ref, c1_ref, ab2_ref, c2_ref, k_ref, v_ref, cache_ref, out_ref):
    index = index_ref[0]
    last = pl.program_id(0) == pl.num_programs(0) - 1
    rows, hd = k_ref.shape
    q = jnp.concatenate(
        [jnp.where(last, c1_ref[0], ab1_ref[0]), jnp.where(last, c2_ref[0], ab2_ref[0])], 0
    )
    both = 2 * rows
    blocks = cache_ref.shape[1] // rows
    wrapped = index >= blocks
    row = lax.rem(lax.broadcasted_iota(jnp.int32, (both, rows), 0), rows)
    col = lax.broadcasted_iota(jnp.int32, (both, rows), 1)
    own = col <= row
    starts, scores, shifts = [], [], []
    top = None
    for rel in range(blocks):
        block = lax.rem(index + rel, blocks)
        start = pl.multiple_of(block * rows, rows)
        starts.append(start)
        s = dot_t(q, cache_ref[0, pl.ds(start, rows), :hd])
        if rel == 0:
            s = jnp.where(own, dot_t(q, k_ref[...]), jnp.where(wrapped, s, NEG))
            shift = jnp.float32(0)
        else:
            shift = jnp.where(wrapped | (block < index), jnp.float32(0), jnp.float32(NEG))
        scores.append(s)
        shifts.append(shift)
        peak = jnp.max(s, 1, keepdims=True) + shift
        top = peak if top is None else jnp.maximum(top, peak)
    scale = LOG2E * hd**-0.5
    base = top * scale
    total = jnp.zeros((both, 1), F32)
    mixed = jnp.zeros((both, hd), F32)
    for rel in range(blocks):
        terms = jnp.exp2(scores[rel] * scale - (base - shifts[rel]))
        total += jnp.sum(terms, 1, keepdims=True)
        old_values = cache_ref[0, pl.ds(starts[rel], rows), hd:]
        if rel == 0:
            mixed += dot(jnp.where(own, terms, 0.0).astype(BF16), v_ref[...])
            mixed += dot(jnp.where(own, 0.0, terms).astype(BF16), old_values)
        else:
            mixed += dot(terms.astype(BF16), old_values)
    made = (mixed / total).astype(BF16)
    out_ref[0] = made[:rows]
    out_ref[1] = made[rows:]


def span_attend(index, ours, theirs, key, value, rows, cache):
    half, hd = ours[0].shape[0] + 1, ours[0].shape[2]
    heads = 2 * half
    window = cache.shape[1]
    many = pl.BlockSpec((1, rows, hd), lambda h, s: (jnp.minimum(h, half - 2), 0, 0))
    single = pl.BlockSpec((1, rows, hd), lambda h, s: (0, 0, 0))
    pair = pl.BlockSpec((rows, hd), lambda h, s: (0, 0))
    return pl.pallas_call(
        span_body,
        grid_spec=pltpu.PrefetchScalarGridSpec(
            num_scalar_prefetch=1,
            grid=(half,),
            in_specs=[many, single, many, single, pair, pair]
            + [pl.BlockSpec((1, window, 2 * hd), lambda h, s: (0, 0, 0))],
            out_specs=pl.BlockSpec((2, rows, hd), lambda h, s: (0, 0, h)),
        ),
        out_shape=jax.ShapeDtypeStruct((2, rows, half * hd), BF16),
        compiler_params=params(36, "arbitrary"),
        cost_estimate=pl.CostEstimate(
            flops=4 * heads * rows * hd * (window + rows),
            bytes_accessed=4 * hd * window,
            transcendentals=heads * rows * window,
        ),
        name="span_attend",
    )(index, *ours, *theirs, key, value, cache)


def finish_body(
    info_ref, att_ref, datt_ref, x_ref, dx_ref, *refs
):
    chunks, (out_ref, dout_ref, lhs, w, sem) = refs[:16], refs[16:]
    rows, k = att_ref.shape[1:]
    step = pl.program_id(0)
    core = info_ref[0]

    def copies(quarter):
        for i in range(4):
            place = info_ref[1 + quarter * 4 + i]
            if quarter % 2:
                to = w.at[quarter, place]
            else:
                to = w.at[quarter, :, :, place]
            yield pltpu.make_async_copy(chunks[quarter * 4 + i], to, sem.at[quarter, i])

    @pl.when(step == 0)
    def _():
        for quarter in range(4):
            for copy in copies(quarter):
                copy.start()
        lhs[core, :rows] = att_ref[0]
        lhs[1 - core, :rows] = att_ref[1]
        lhs[0, rows:] = datt_ref[:, :k]
        lhs[1, rows:] = datt_ref[:, k:]

    for quarter in range(4):

        @pl.when(step == quarter)
        def _():
            for copy in copies(quarter):
                copy.wait()

    total = None
    for half in range(2):
        right = w[step, 2 * half : 2 * half + 2].reshape(k, w.shape[-1])
        term = dot(lhs[half], right)
        total = term if total is None else total + term
    out_ref[...] = (x_ref[...].astype(F32) + total[:rows]).astype(BF16)
    drows = dx_ref.shape[0]
    dout_ref[...] = (dx_ref[...].astype(F32) + total[rows : rows + drows]).astype(BF16)


def finish(info, att, datt, x, dx, chunks):
    rows, n = x.shape
    drows = dx.shape[0]
    run, bn = chunks[0].shape[2:]

    def column(i, s):
        return 0, lax.rem(s[0] * 2 + i, 4)

    return pl.pallas_call(
        finish_body,
        grid_spec=pltpu.PrefetchScalarGridSpec(
            num_scalar_prefetch=1,
            grid=(4,),
            in_specs=[
                pl.BlockSpec(att.shape, lambda i, s: (0, 0, 0)),
                pl.BlockSpec(datt.shape, lambda i, s: (0, 0)),
                pl.BlockSpec((rows, bn), column),
                pl.BlockSpec((drows, bn), column),
            ]
            + [pl.BlockSpec(memory_space=pl.ANY)] * 16,
            out_specs=[pl.BlockSpec((rows, bn), column), pl.BlockSpec((drows, bn), column)],
            scratch_shapes=[
                pltpu.VMEM((2, rows + EXTRA, n // 2), BF16),
                pltpu.VMEM((4, 4, 2, 4, run, bn), BF16),
                pltpu.SemaphoreType.DMA((4, 4)),
            ],
        ),
        out_shape=[
            jax.ShapeDtypeStruct((rows, n), BF16),
            jax.ShapeDtypeStruct((drows, n), BF16),
        ],
        compiler_params=params(24, "arbitrary"),
        cost_estimate=pl.CostEstimate(
            flops=2 * rows * n * n, bytes_accessed=2 * n * n, transcendentals=0
        ),
        name="finish",
    )(info, att, datt, x, dx, *chunks)


def exchange(sent, axes):
    members = lax.axis_size(axes)
    got = lax.all_to_all(sent.reshape((members, -1) + sent.shape[1:]), axes, 0, 0)
    return got.reshape(sent.shape)


STRIDE = {"y": 32, "x": 4, "z": 1}
DEVICES = np.arange(128)


def spot(axis):
    return DEVICES // STRIDE[axis] % 4


def send(v, axis, by):
    at = spot(axis)
    to = DEVICES + ((at + by) % 4 - at) * STRIDE[axis]
    return lax.ppermute(v, AXES, list(zip(DEVICES.tolist(), to.tolist())))


def swap(v):
    return lax.ppermute(v, AXES, list(zip(DEVICES.tolist(), (DEVICES ^ 16).tolist())))


RING = np.where(DEVICES // 16 % 2 == 0, 1, 3)


def put(whole, piece, index, place):
    start = [jnp.uint32(0)] * whole.ndim
    start[place] = index
    return lax.dynamic_update_slice(whole, jnp.expand_dims(piece, place), start)


def shards(
    devices,
    span_tokens,
    decode_tokens,
    norm_gain,
    query_weight,
    keyval_weight,
    output_weight,
    span_cache,
    decode_cache,
    span_index,
    decode_length,
    cache_slot,
):
    rows, width = span_tokens.shape[1:]
    own = decode_cache.shape[0]
    hd = keyval_weight.shape[1] // 2
    device = lax.axis_index(AXES).astype(jnp.uint32)
    core = ((device >> 4) & 1).astype(jnp.int32)
    first_core = core == 0
    run = query_weight.shape[0]

    half_q, half_kv = width // 2, hd
    halves = [
        jnp.concatenate(
            [
                query_weight[:, i * half_q : (i + 1) * half_q],
                keyval_weight[:, i * half_kv : (i + 1) * half_kv],
                output_weight[:, i * half_q : (i + 1) * half_q],
            ],
            1,
        )
        for i in range(2)
    ]
    got = swap(jnp.where(first_core, halves[1], halves[0]))
    piece = jnp.where(
        first_core, jnp.concatenate([halves[0], got], 0), jnp.concatenate([got, halves[1]], 0)
    )
    places = devices * own
    slots_here = (device * own).astype(jnp.int32) + jnp.arange(own, dtype=jnp.int32)
    slot_of_mine = lax.dynamic_slice(cache_slot, (device * own,), (own,))
    request_of_mine = jnp.argmax(cache_slot[None, :] == slots_here[:, None], 1).astype(jnp.int32)
    digits = jnp.stack([decode_length // 256, decode_length % 256], 1).astype(BF16)
    tagged = jnp.concatenate([decode_tokens, jnp.pad(digits, ((0, 0), (0, 510)))], 1)
    tagged = tagged.reshape(own, SLAB, 128)
    tagged = jnp.broadcast_to(tagged, (8,) + tagged.shape).reshape(8 * own, SLAB, 128)
    split = half_q + half_kv
    first_weight = lax.all_gather(piece[:, :split], CHIPS, axis=0, tiled=True)

    here = {axis: (device >> shift) & 3 for axis, shift in (("y", 5), ("x", 2), ("z", 0))}
    back = 1 - 2 * ((device >> 4) & 1)
    came = {axis: [(at - back * k) & 3 for k in range(4)] for axis, at in here.items()}
    strip = piece[:, split:]
    strips = [strip] + [send(strip, "z", k) for k in (1, 2, 3)]
    tagged, _ = lax.optimization_barrier((tagged, strips))
    tagged = place(cache_slot, device.astype(jnp.int32)[None], exchange(tagged, ("c", "z")))
    strips = interleave(here["z"].astype(jnp.int32)[None], strips)
    bn = half_q // 2
    stack = [strips[:, :, :bn], strips[:, :, bn:]]
    plan = (("y", 0, "x", 2), ("x", 1, "y", 0))
    parts = [
        jnp.zeros((4, 2, 4 * run, bn), BF16),
        jnp.zeros((2, 4, 4 * run, bn), BF16),
    ]
    for k in range(4):
        for i, (axis, dim, _, _) in enumerate(plan):
            stack[i] = send(stack[i], axis, RING) if k else stack[i]
            parts[i] = put(parts[i], stack[i], came[axis][k], dim)
    arrived = pick(exchange(tagged, ("y", "x")), request_of_mine, by_chip)
    arrived = arrived.reshape(own, SLAB * 128)
    own_tokens = jnp.pad(arrived[:, :width], ((0, EXTRA - own), (0, 0)))
    tags = arrived[:, width : width + 2].astype(jnp.int32)
    own_length = tags[:, 0] * 256 + tags[:, 1]

    offset = span_index[0] * rows
    span_positions = offset + jnp.arange(rows, dtype=jnp.int32)
    decode_positions = jnp.pad(own_length, (0, EXTRA - own))
    positions = jnp.concatenate(
        [span_positions, swap(span_positions), decode_positions, swap(decode_positions)]
    )
    quarter = hd // 4
    frequency = 10000.0 ** (-jnp.arange(quarter, dtype=F32) / quarter)
    angles = positions.astype(F32)[:, None] * frequency
    cos, sin = jnp.cos(angles), jnp.sin(angles)
    cos = jnp.concatenate([cos, cos], 1)
    sin = jnp.concatenate([-sin, sin], 1)
    cos = jnp.stack([cos, jnp.where(first_core, cos, 1.0)])
    sin = jnp.stack([sin, jnp.where(first_core, sin, 0.0)])

    order = arrival_order(run)
    both_spans = jnp.concatenate([span_tokens[0], swap(span_tokens[0])], 0)
    both_decodes = jnp.concatenate([own_tokens, swap(own_tokens)], 0)
    total = 2 * (rows + EXTRA)
    lhs = norm_ordered(both_spans, norm_gain, order, total, 128, 0)
    at = 2 * rows // (2 * EXTRA)
    lhs = norm_ordered(both_decodes, norm_gain, order, total, 2 * EXTRA, at, (lhs,))
    mine = [[part] for part in parts]
    theirs = [[swap(part)] for part in parts]
    def ring_step(parts):
        parts = [send(part, p[2], RING) for part, p in zip(parts, plan)]
        for i in range(2):
            mine[i].append(parts[i])
        return parts

    def swap_last(after):
        parts, _ = lax.optimization_barrier(([m[-1] for m in mine], after))
        for i in range(2):
            theirs[i].append(swap(parts[i]))

    parts = ring_step(parts)
    swap_last(())
    shifts = jnp.asarray([2] * 4 + [5] * 4 + [2] * 4 + [5] * 4, jnp.int32)
    steps = jnp.asarray([0, 1, 2, 3] * 2 + [0, -1, -2, -3] * 2, jnp.int32)
    came_from = (((device.astype(jnp.int32) >> shifts) & 3) - (1 - 2 * core) * steps) & 3
    finish_info = jnp.concatenate([core[None], came_from])
    info = jnp.concatenate([own_length, request_of_mine, core[None]])
    parts, lhs, cos, sin, finish_info, info = lax.optimization_barrier(
        (parts, lhs, cos, sin, finish_info, info)
    )
    ring_step(parts)
    first_weight, cos, sin = (
        pltpu.with_memory_space_constraint(v, pltpu.HBM) for v in (first_weight, cos, sin)
    )
    ours_c, other_c = project(4, 2, rows, lhs, first_weight, cos, sin, hd)
    theirs_c = swap(other_c)
    ours_ab, other_ab = project(0, 4, rows, lhs, first_weight, cos, sin, hd)
    theirs_ab = swap(other_ab)
    swap_last(ours_ab)
    parts, _ = lax.optimization_barrier(([m[-1] for m in mine], ours_ab))
    ring_step(parts)

    key = jnp.where(first_core, ours_c[1], theirs_c[1])
    value = jnp.where(first_core, theirs_c[1], ours_c[1])
    keyval = jnp.concatenate([key, value], 1)
    decode_keyval = keyval[rows : rows + own]
    quarters = (ours_ab, ours_c, theirs_ab, theirs_c)
    routed = decode_attend(info, quarters, keyval, decode_cache, places)
    home = exchange(routed, AXES)
    swap_last(routed)
    att = span_attend(
        span_index, (ours_ab, ours_c), (theirs_ab, theirs_c), key, value, rows, span_cache
    )
    home = pick(home, slot_of_mine, by_device).reshape(own, SLAB * 128)[:, :width]
    span_output, decode_output = finish(
        finish_info,
        att,
        jnp.pad(home, ((0, EXTRA - own), (0, 0))),
        span_tokens[0],
        decode_tokens,
        [c for half in (mine, theirs) for part in half for c in part],
    )
    return span_output[None], keyval[:rows][None], decode_output, decode_keyval


def solution(mesh):
    both = P(AXES)
    return jax.shard_map(
        functools.partial(shards, mesh.size),
        mesh=Mesh(mesh.devices.reshape(4, 2, 4, 4), AXES),
        in_specs=(both, both, P(), both, both, both, both, both, both, both, P()),
        out_specs=(both, both, both, both),
        check_vma=False,
    )
```

```python
import functools

import jax
import jax.numpy as jnp
import numpy as np
from jax import lax
from jax.experimental import pallas as pl
from jax.experimental.pallas import tpu as pltpu
from jax.sharding import Mesh
from jax.sharding import PartitionSpec as P

AXES = ("y", "c", "x", "z")
CHIPS = ("y", "x", "z")
LOG2E = 1.4426950408889634
NEG = -1e30
F32 = jnp.float32
BF16 = jnp.bfloat16
EXTRA = 16


def params(mib, *semantics):
    return pltpu.CompilerParams(vmem_limit_bytes=mib << 20, dimension_semantics=semantics or None)


def dot(a, b):
    return jnp.dot(a, b, preferred_element_type=F32)


def dot_t(a, b):
    return lax.dot_general(a, b, (((1,), (1,)), ((), ())), preferred_element_type=F32)


def mover(to, width):
    return (jnp.asarray(to, jnp.int32)[:, None] == jnp.arange(width)[None, :]).astype(BF16)


def arrival_order(run):
    core, x, z, r = np.meshgrid(*(np.arange(n) for n in (2, 4, 4, run)), indexing="ij")
    return mover((((x * 4 + z) * 2 + core) * run + r).reshape(-1), 32 * run)


def norm_body(x_ref, gain_ref, order_ref, *refs):
    out_ref = refs[-1]
    x = x_ref[...].astype(F32)
    rows = x.shape[0]
    mean = jnp.mean(x * x, axis=-1, keepdims=True)
    normed = (x * lax.rsqrt(mean + 1e-06) * gain_ref[...]).astype(BF16)
    k = order_ref.shape[0]
    blocks = jnp.concatenate([normed[:, y * k : (y + 1) * k] for y in range(4)], 0)
    moved = dot(blocks, order_ref[...]).astype(BF16)
    for y in range(4):
        out_ref[:, y * k : (y + 1) * k] = moved[y * rows : (y + 1) * rows]


def norm_ordered(x, gain, order, total, block, at, into=()):
    rows, width = x.shape
    return pl.pallas_call(
        norm_body,
        grid=(rows // block,),
        in_specs=[
            pl.BlockSpec((block, width), lambda i: (i, 0)),
            pl.BlockSpec((1, width), lambda i: (0, 0)),
            pl.BlockSpec(order.shape, lambda i: (0, 0)),
        ]
        + [pl.BlockSpec(memory_space=pl.ANY)] * len(into),
        out_specs=pl.BlockSpec((block, width), lambda i: (at + i, 0)),
        out_shape=jax.ShapeDtypeStruct((total, width), BF16),
        input_output_aliases={3 + i: i for i in range(len(into))},
        compiler_params=params(24, "arbitrary"),
        cost_estimate=pl.CostEstimate(
            flops=2 * rows * width * 640, bytes_accessed=4 * rows * width, transcendentals=0
        ),
        name="norm_ordered",
    )(x, gain[None], order, *into)


def rotate(v, cos_ref, sin_ref):
    half = v[:, :128]
    turned = half * cos_ref[...] + pltpu.roll(half, 64, 1) * sin_ref[...]
    return jnp.concatenate([turned, v[:, 128:]], 1)


def project_body(rows, x_ref, w_ref, cos_ref, sin_ref, ours_ref, other_ref):
    extra = ours_ref.shape[1] - rows
    made = rotate(dot(x_ref[...], w_ref[...]), cos_ref.at[0], sin_ref.at[0]).astype(BF16)
    ours_ref[0, :rows] = made[:rows]
    other_ref[0, :rows] = made[rows : 2 * rows]
    ours_ref[0, rows:] = made[2 * rows : 2 * rows + extra]
    other_ref[0, rows:] = made[2 * rows + extra :]


def project(first, count, rows, x, w, cos, sin, hd):
    total, depth = x.shape
    last = w.shape[1] // hd - 1
    shape = jax.ShapeDtypeStruct((count, total // 2, hd), BF16)
    table = pl.BlockSpec((1, total, 128), lambda i: ((first + i) // last, 0, 0))
    return pl.pallas_call(
        functools.partial(project_body, rows),
        grid=(count,),
        in_specs=[
            pl.BlockSpec((total, depth), lambda i: (0, 0)),
            pl.BlockSpec((depth, hd), lambda i: (0, first + i)),
            table,
            table,
        ],
        out_specs=[pl.BlockSpec((1, total // 2, hd), lambda i: (i, 0, 0))] * 2,
        out_shape=[shape, shape],
        compiler_params=params(32, "arbitrary"),
        cost_estimate=pl.CostEstimate(
            flops=2 * total * count * depth * hd,
            bytes_accessed=2 * count * depth * hd,
            transcendentals=0,
        ),
        name="project",
    )(x, w, cos, sin)


SLAB = 24


def decode_body(
    info_ref, oab_ref, oc_ref, tab_ref, tc_ref, own_ref, cache_ref, out_ref, gather_ref, spill_ref
):
    i = pl.program_id(0)
    length, to, core = info_ref[i], info_ref[2 + i], info_ref[4]
    hd = cache_ref.shape[2] // 2
    window = cache_ref.shape[1]
    for half, (ab_ref, c_ref) in enumerate(((oab_ref, oc_ref), (tab_ref, tc_ref))):
        for h in range(5):
            block = ab_ref[h] if h < 4 else c_ref[0]
            block = block.astype(F32)
            row = jnp.where(i == 0, block[0:1], block[1:2])
            gather_ref[half * 5 + h : half * 5 + h + 1] = row
    gather_ref[10:16] = jnp.zeros((6, hd), F32)
    q = gather_ref[...].astype(BF16)
    scores = dot_t(q, cache_ref[0, :, :hd])
    own_row = own_ref[...].astype(F32)
    own_row = jnp.where(i == 0, own_row[0:1], own_row[1:2])
    own = jnp.sum(gather_ref[...] * own_row[:, :hd], axis=1, keepdims=True)
    slot = lax.broadcasted_iota(jnp.int32, scores.shape, 1)
    met = (slot < length) & (slot != lax.rem(length, window))
    scores = jnp.where(met, scores, NEG)
    top = jnp.maximum(jnp.max(scores, 1, keepdims=True), own)
    scale = LOG2E * hd**-0.5
    terms = jnp.where(met, jnp.exp2((scores - top) * scale), 0.0)
    own_term = jnp.exp2((own - top) * scale)
    total = jnp.sum(terms, 1, keepdims=True) + own_term
    weights = (terms / total).astype(BF16)
    own_weight = (own_term / total).astype(BF16).astype(F32)
    mixed = dot(weights, cache_ref[0, :, hd:]) + own_weight * own_row[:, hd:]
    spill_ref[20:] = jnp.zeros((SLAB - 20, 128), F32)
    for h in range(10):
        head = jnp.where(core == 0, h, (h + 5) % 10)
        for part in range(2):
            spill_ref[pl.ds(2 * head + part, 1)] = mixed[h : h + 1, part * 128 : part * 128 + 128]
    out_ref[to] = spill_ref[...].astype(BF16)


def decode_attend(info, parts, own, cache, places):
    n, window, wide = cache.shape
    hd = wide // 2
    last = parts[0].shape[1] // EXTRA - 1
    return pl.pallas_call(
        decode_body,
        grid_spec=pltpu.PrefetchScalarGridSpec(
            num_scalar_prefetch=1,
            grid=(n,),
            in_specs=[
                pl.BlockSpec((p.shape[0], EXTRA, hd), lambda i, s: (0, last, 0)) for p in parts
            ]
            + [
                pl.BlockSpec((EXTRA, wide), lambda i, s: (last, 0)),
                pl.BlockSpec((1, window, wide), lambda i, s: (i, 0, 0)),
            ],
            out_specs=pl.BlockSpec((places, SLAB, 128), lambda i, s: (0, 0, 0)),
            scratch_shapes=[pltpu.VMEM((16, hd), F32), pltpu.VMEM((SLAB, 128), F32)],
        ),
        out_shape=jax.ShapeDtypeStruct((places, SLAB, 128), BF16),
        compiler_params=params(24, "arbitrary"),
        cost_estimate=pl.CostEstimate(
            flops=64 * n * hd * window, bytes_accessed=4 * n * hd * window, transcendentals=0
        ),
        name="decode_attend",
    )(info, *parts, own, cache)


def interleave_body(z_ref, *refs):
    pieces, out_ref = refs[:4], refs[4]
    run = pieces[0].shape[0] // 2
    for z in range(4):

        @pl.when(z_ref[0] == z)
        def _():
            for core in range(2):
                rows = [
                    pieces[(z - at) % 4][core * run : (core + 1) * run].astype(F32) for at in range(4)
                ]
                out_ref[core] = jnp.concatenate(rows, 0).astype(BF16)


def interleave(z, pieces):
    rows, cols = pieces[0].shape
    vmem = pl.BlockSpec(memory_space=pltpu.VMEM)
    return pl.pallas_call(
        interleave_body,
        in_specs=[pl.BlockSpec(memory_space=pltpu.SMEM)] + [vmem] * 4,
        out_specs=vmem,
        out_shape=jax.ShapeDtypeStruct((2, 2 * rows, cols), BF16),
        compiler_params=params(8),
        name="interleave",
    )(z, *pieces)


def place_body(slot_ref, here_ref, rows_ref, out_ref):
    here = here_ref[0]
    for i in range(rows_ref.shape[0]):
        core, z, each = i // 8, i // 2 % 4, i % 2
        source = (here & 0b1101100) | (core * 16 + z)
        slot = slot_ref[source * 2 + each]
        to = slot >> 1

        @pl.when((to & 0b0010011) == (here & 0b0010011))
        def _():
            chip = ((to >> 5) << 2) | ((to >> 2) & 3)
            out_ref[chip * 2 + (slot & 1)] = rows_ref[i]


def place(slots, here, rows):
    smem = pl.BlockSpec(memory_space=pltpu.SMEM)
    vmem = pl.BlockSpec(memory_space=pltpu.VMEM)
    return pl.pallas_call(
        place_body,
        in_specs=[smem, smem, vmem],
        out_specs=vmem,
        out_shape=jax.ShapeDtypeStruct((32,) + rows.shape[1:], BF16),
        compiler_params=params(8),
        name="place",
    )(slots, here, rows)


def pick_body(came_ref, slab_ref, out_ref):
    out_ref[...] = slab_ref[...]


def by_device(came):
    return came >> 1


def by_chip(came):
    return ((came >> 6) << 2) | ((came >> 3) & 3)


def pick(arrived, came_from, where):
    slab = arrived.shape[1:]
    return pl.pallas_call(
        pick_body,
        grid_spec=pltpu.PrefetchScalarGridSpec(
            num_scalar_prefetch=1,
            grid=(2,),
            in_specs=[
                pl.BlockSpec((1,) + slab, lambda i, s: (where(s[i]) * 2 + i, 0, 0))
            ],
            out_specs=pl.BlockSpec((1,) + slab, lambda i, s: (i, 0, 0)),
        ),
        out_shape=jax.ShapeDtypeStruct((2,) + slab, BF16),
        compiler_params=params(8, "arbitrary"),
        name="pick",
    )(came_from, arrived)


def span_body(index_ref, ab1_ref, c1_ref, ab2_ref, c2_ref, k_ref, v_ref, cache_ref, out_ref):
    index = index_ref[0]
    last = pl.program_id(0) == pl.num_programs(0) - 1
    rows, hd = k_ref.shape
    q = jnp.concatenate(
        [jnp.where(last, c1_ref[0], ab1_ref[0]), jnp.where(last, c2_ref[0], ab2_ref[0])], 0
    )
    both = 2 * rows
    blocks = cache_ref.shape[1] // rows
    wrapped = index >= blocks
    row = lax.rem(lax.broadcasted_iota(jnp.int32, (both, rows), 0), rows)
    col = lax.broadcasted_iota(jnp.int32, (both, rows), 1)
    own = col <= row
    starts, scores, shifts = [], [], []
    top = None
    for rel in range(blocks):
        block = lax.rem(index + rel, blocks)
        start = pl.multiple_of(block * rows, rows)
        starts.append(start)
        s = dot_t(q, cache_ref[0, pl.ds(start, rows), :hd])
        if rel == 0:
            s = jnp.where(own, dot_t(q, k_ref[...]), jnp.where(wrapped, s, NEG))
            shift = jnp.float32(0)
        else:
            shift = jnp.where(wrapped | (block < index), jnp.float32(0), jnp.float32(NEG))
        scores.append(s)
        shifts.append(shift)
        peak = jnp.max(s, 1, keepdims=True) + shift
        top = peak if top is None else jnp.maximum(top, peak)
    scale = LOG2E * hd**-0.5
    base = top * scale
    total = jnp.zeros((both, 1), F32)
    mixed = jnp.zeros((both, hd), F32)
    for rel in range(blocks):
        terms = jnp.exp2(scores[rel] * scale - (base - shifts[rel]))
        total += jnp.sum(terms, 1, keepdims=True)
        old_values = cache_ref[0, pl.ds(starts[rel], rows), hd:]
        if rel == 0:
            mixed += dot(jnp.where(own, terms, 0.0).astype(BF16), v_ref[...])
            mixed += dot(jnp.where(own, 0.0, terms).astype(BF16), old_values)
        else:
            mixed += dot(terms.astype(BF16), old_values)
    made = (mixed / total).astype(BF16)
    out_ref[0] = made[:rows]
    out_ref[1] = made[rows:]


def span_attend(index, ours, theirs, key, value, rows, cache):
    half, hd = ours[0].shape[0] + 1, ours[0].shape[2]
    heads = 2 * half
    window = cache.shape[1]
    many = pl.BlockSpec((1, rows, hd), lambda h, s: (jnp.minimum(h, half - 2), 0, 0))
    single = pl.BlockSpec((1, rows, hd), lambda h, s: (0, 0, 0))
    pair = pl.BlockSpec((rows, hd), lambda h, s: (0, 0))
    return pl.pallas_call(
        span_body,
        grid_spec=pltpu.PrefetchScalarGridSpec(
            num_scalar_prefetch=1,
            grid=(half,),
            in_specs=[many, single, many, single, pair, pair]
            + [pl.BlockSpec((1, window, 2 * hd), lambda h, s: (0, 0, 0))],
            out_specs=pl.BlockSpec((2, rows, hd), lambda h, s: (0, 0, h)),
        ),
        out_shape=jax.ShapeDtypeStruct((2, rows, half * hd), BF16),
        compiler_params=params(36, "arbitrary"),
        cost_estimate=pl.CostEstimate(
            flops=4 * heads * rows * hd * (window + rows),
            bytes_accessed=4 * hd * window,
            transcendentals=heads * rows * window,
        ),
        name="span_attend",
    )(index, *ours, *theirs, key, value, cache)


def finish_body(
    info_ref, att_ref, datt_ref, x_ref, dx_ref, *refs
):
    chunks, (out_ref, dout_ref, lhs, w, sem) = refs[:16], refs[16:]
    rows, k = att_ref.shape[1:]
    step = pl.program_id(0)
    core = info_ref[0]

    def copies(quarter):
        for i in range(4):
            place = info_ref[1 + quarter * 4 + i]
            if quarter % 2:
                to = w.at[quarter, place]
            else:
                to = w.at[quarter, :, :, place]
            yield pltpu.make_async_copy(chunks[quarter * 4 + i], to, sem.at[quarter, i])

    @pl.when(step == 0)
    def _():
        for quarter in range(4):
            for copy in copies(quarter):
                copy.start()
        lhs[core, :rows] = att_ref[0]
        lhs[1 - core, :rows] = att_ref[1]
        lhs[0, rows:] = datt_ref[:, :k]
        lhs[1, rows:] = datt_ref[:, k:]

    for quarter in range(4):

        @pl.when(step == quarter)
        def _():
            for copy in copies(quarter):
                copy.wait()

    total = None
    for half in range(2):
        right = w[step, 2 * half : 2 * half + 2].reshape(k, w.shape[-1])
        term = dot(lhs[half], right)
        total = term if total is None else total + term
    out_ref[...] = (x_ref[...].astype(F32) + total[:rows]).astype(BF16)
    drows = dx_ref.shape[0]
    dout_ref[...] = (dx_ref[...].astype(F32) + total[rows : rows + drows]).astype(BF16)


def finish(info, att, datt, x, dx, chunks):
    rows, n = x.shape
    drows = dx.shape[0]
    run, bn = chunks[0].shape[2:]

    def column(i, s):
        return 0, lax.rem(s[0] * 2 + i, 4)

    return pl.pallas_call(
        finish_body,
        grid_spec=pltpu.PrefetchScalarGridSpec(
            num_scalar_prefetch=1,
            grid=(4,),
            in_specs=[
                pl.BlockSpec(att.shape, lambda i, s: (0, 0, 0)),
                pl.BlockSpec(datt.shape, lambda i, s: (0, 0)),
                pl.BlockSpec((rows, bn), column),
                pl.BlockSpec((drows, bn), column),
            ]
            + [pl.BlockSpec(memory_space=pl.ANY)] * 16,
            out_specs=[pl.BlockSpec((rows, bn), column), pl.BlockSpec((drows, bn), column)],
            scratch_shapes=[
                pltpu.VMEM((2, rows + EXTRA, n // 2), BF16),
                pltpu.VMEM((4, 4, 2, 4, run, bn), BF16),
                pltpu.SemaphoreType.DMA((4, 4)),
            ],
        ),
        out_shape=[
            jax.ShapeDtypeStruct((rows, n), BF16),
            jax.ShapeDtypeStruct((drows, n), BF16),
        ],
        compiler_params=params(60, "arbitrary"),
        cost_estimate=pl.CostEstimate(
            flops=2 * rows * n * n, bytes_accessed=2 * n * n, transcendentals=0
        ),
        name="finish",
    )(info, att, datt, x, dx, *chunks)


def exchange(sent, axes):
    members = lax.axis_size(axes)
    got = lax.all_to_all(sent.reshape((members, -1) + sent.shape[1:]), axes, 0, 0)
    return got.reshape(sent.shape)


STRIDE = {"y": 32, "x": 4, "z": 1}
DEVICES = np.arange(128)


def spot(axis):
    return DEVICES // STRIDE[axis] % 4


def send(v, axis, by):
    at = spot(axis)
    to = DEVICES + ((at + by) % 4 - at) * STRIDE[axis]
    return lax.ppermute(v, AXES, list(zip(DEVICES.tolist(), to.tolist())))


def swap(v):
    return lax.ppermute(v, AXES, list(zip(DEVICES.tolist(), (DEVICES ^ 16).tolist())))


RING = np.where(DEVICES // 16 % 2 == 0, 1, 3)


def put(whole, piece, index, place):
    start = [jnp.uint32(0)] * whole.ndim
    start[place] = index
    return lax.dynamic_update_slice(whole, jnp.expand_dims(piece, place), start)


def shards(
    devices,
    span_tokens,
    decode_tokens,
    norm_gain,
    query_weight,
    keyval_weight,
    output_weight,
    span_cache,
    decode_cache,
    span_index,
    decode_length,
    cache_slot,
):
    rows, width = span_tokens.shape[1:]
    own = decode_cache.shape[0]
    hd = keyval_weight.shape[1] // 2
    device = lax.axis_index(AXES).astype(jnp.uint32)
    core = ((device >> 4) & 1).astype(jnp.int32)
    first_core = core == 0
    run = query_weight.shape[0]

    half_q, half_kv = width // 2, hd
    halves = [
        jnp.concatenate(
            [
                query_weight[:, i * half_q : (i + 1) * half_q],
                keyval_weight[:, i * half_kv : (i + 1) * half_kv],
                output_weight[:, i * half_q : (i + 1) * half_q],
            ],
            1,
        )
        for i in range(2)
    ]
    got = swap(jnp.where(first_core, halves[1], halves[0]))
    piece = jnp.where(
        first_core, jnp.concatenate([halves[0], got], 0), jnp.concatenate([got, halves[1]], 0)
    )
    places = devices * own
    slots_here = (device * own).astype(jnp.int32) + jnp.arange(own, dtype=jnp.int32)
    slot_of_mine = lax.dynamic_slice(cache_slot, (device * own,), (own,))
    request_of_mine = jnp.argmax(cache_slot[None, :] == slots_here[:, None], 1).astype(jnp.int32)
    digits = jnp.stack([decode_length // 256, decode_length % 256], 1).astype(BF16)
    tagged = jnp.concatenate([decode_tokens, jnp.pad(digits, ((0, 0), (0, 510)))], 1)
    tagged = tagged.reshape(own, SLAB, 128)
    tagged = jnp.broadcast_to(tagged, (8,) + tagged.shape).reshape(8 * own, SLAB, 128)
    split = half_q + half_kv
    first_weight = lax.all_gather(piece[:, :split], CHIPS, axis=0, tiled=True)

    here = {axis: (device >> shift) & 3 for axis, shift in (("y", 5), ("x", 2), ("z", 0))}
    back = 1 - 2 * ((device >> 4) & 1)
    came = {axis: [(at - back * k) & 3 for k in range(4)] for axis, at in here.items()}
    strip = piece[:, split:]
    strips = [strip] + [send(strip, "z", k) for k in (1, 2, 3)]
    tagged, _ = lax.optimization_barrier((tagged, strips))
    tagged = place(cache_slot, device.astype(jnp.int32)[None], exchange(tagged, ("c", "z")))
    strips = interleave(here["z"].astype(jnp.int32)[None], strips)
    bn = half_q // 2
    stack = [strips[:, :, :bn], strips[:, :, bn:]]
    plan = (("y", 0, "x", 2), ("x", 1, "y", 0))
    parts = [
        jnp.zeros((4, 2, 4 * run, bn), BF16),
        jnp.zeros((2, 4, 4 * run, bn), BF16),
    ]
    for k in range(4):
        for i, (axis, dim, _, _) in enumerate(plan):
            stack[i] = send(stack[i], axis, RING) if k else stack[i]
            parts[i] = put(parts[i], stack[i], came[axis][k], dim)
    arrived = pick(exchange(tagged, ("y", "x")), request_of_mine, by_chip)
    arrived = arrived.reshape(own, SLAB * 128)
    own_tokens = jnp.pad(arrived[:, :width], ((0, EXTRA - own), (0, 0)))
    tags = arrived[:, width : width + 2].astype(jnp.int32)
    own_length = tags[:, 0] * 256 + tags[:, 1]

    offset = span_index[0] * rows
    span_positions = offset + jnp.arange(rows, dtype=jnp.int32)
    decode_positions = jnp.pad(own_length, (0, EXTRA - own))
    positions = jnp.concatenate(
        [span_positions, swap(span_positions), decode_positions, swap(decode_positions)]
    )
    quarter = hd // 4
    frequency = 10000.0 ** (-jnp.arange(quarter, dtype=F32) / quarter)
    angles = positions.astype(F32)[:, None] * frequency
    cos, sin = jnp.cos(angles), jnp.sin(angles)
    cos = jnp.concatenate([cos, cos], 1)
    sin = jnp.concatenate([-sin, sin], 1)
    cos = jnp.stack([cos, jnp.where(first_core, cos, 1.0)])
    sin = jnp.stack([sin, jnp.where(first_core, sin, 0.0)])

    order = arrival_order(run)
    both_spans = jnp.concatenate([span_tokens[0], swap(span_tokens[0])], 0)
    both_decodes = jnp.concatenate([own_tokens, swap(own_tokens)], 0)
    total = 2 * (rows + EXTRA)
    lhs = norm_ordered(both_spans, norm_gain, order, total, 128, 0)
    at = 2 * rows // (2 * EXTRA)
    lhs = norm_ordered(both_decodes, norm_gain, order, total, 2 * EXTRA, at, (lhs,))
    mine = [[part] for part in parts]
    theirs = [[swap(part)] for part in parts]
    def ring_step(parts):
        parts = [send(part, p[2], RING) for part, p in zip(parts, plan)]
        for i in range(2):
            mine[i].append(parts[i])
        return parts

    def swap_last(after):
        parts, _ = lax.optimization_barrier(([m[-1] for m in mine], after))
        for i in range(2):
            theirs[i].append(swap(parts[i]))

    parts = ring_step(parts)
    swap_last(())
    shifts = jnp.asarray([2] * 4 + [5] * 4 + [2] * 4 + [5] * 4, jnp.int32)
    steps = jnp.asarray([0, 1, 2, 3] * 2 + [0, -1, -2, -3] * 2, jnp.int32)
    came_from = (((device.astype(jnp.int32) >> shifts) & 3) - (1 - 2 * core) * steps) & 3
    finish_info = jnp.concatenate([core[None], came_from])
    info = jnp.concatenate([own_length, request_of_mine, core[None]])
    parts, lhs, cos, sin, finish_info, info = lax.optimization_barrier(
        (parts, lhs, cos, sin, finish_info, info)
    )
    ring_step(parts)
    first_weight, cos, sin = (
        pltpu.with_memory_space_constraint(v, pltpu.HBM) for v in (first_weight, cos, sin)
    )
    ours_c, other_c = project(4, 2, rows, lhs, first_weight, cos, sin, hd)
    theirs_c = swap(other_c)
    ours_ab, other_ab = project(0, 4, rows, lhs, first_weight, cos, sin, hd)
    theirs_ab = swap(other_ab)
    swap_last(ours_ab)
    parts, _ = lax.optimization_barrier(([m[-1] for m in mine], ours_ab))
    ring_step(parts)

    key = jnp.where(first_core, ours_c[1], theirs_c[1])
    value = jnp.where(first_core, theirs_c[1], ours_c[1])
    keyval = jnp.concatenate([key, value], 1)
    decode_keyval = keyval[rows : rows + own]
    quarters = (ours_ab, ours_c, theirs_ab, theirs_c)
    routed = decode_attend(info, quarters, keyval, decode_cache, places)
    home = exchange(routed, AXES)
    swap_last(routed)
    att = span_attend(
        span_index, (ours_ab, ours_c), (theirs_ab, theirs_c), key, value, rows, span_cache
    )
    home = pick(home, slot_of_mine, by_device).reshape(own, SLAB * 128)[:, :width]
    span_output, decode_output = finish(
        finish_info,
        att,
        jnp.pad(home, ((0, EXTRA - own), (0, 0))),
        span_tokens[0],
        decode_tokens,
        [c for half in (mine, theirs) for part in half for c in part],
    )
    return span_output[None], keyval[:rows][None], decode_output, decode_keyval


def solution(mesh):
    both = P(AXES)
    return jax.shard_map(
        functools.partial(shards, mesh.size),
        mesh=Mesh(mesh.devices.reshape(4, 2, 4, 4), AXES),
        in_specs=(both, both, P(), both, both, both, both, both, both, both, P()),
        out_specs=(both, both, both, both),
        check_vma=False,
    )
```

```python
import functools

import jax
import jax.numpy as jnp
import numpy as np
from jax import lax
from jax.experimental import pallas as pl
from jax.experimental.pallas import tpu as pltpu
from jax.sharding import Mesh
from jax.sharding import PartitionSpec as P

AXES = ("y", "c", "x", "z")
CHIPS = ("y", "x", "z")
LOG2E = 1.4426950408889634
NEG = -1e30
F32 = jnp.float32
BF16 = jnp.bfloat16
EXTRA = 16


def params(mib, *semantics):
    return pltpu.CompilerParams(vmem_limit_bytes=mib << 20, dimension_semantics=semantics or None)


def dot(a, b):
    return jnp.dot(a, b, preferred_element_type=F32)


def dot_t(a, b):
    return lax.dot_general(a, b, (((1,), (1,)), ((), ())), preferred_element_type=F32)


def mover(to, width):
    return (jnp.asarray(to, jnp.int32)[:, None] == jnp.arange(width)[None, :]).astype(BF16)


def arrival_order(run):
    core, x, z, r = np.meshgrid(*(np.arange(n) for n in (2, 4, 4, run)), indexing="ij")
    return mover((((x * 4 + z) * 2 + core) * run + r).reshape(-1), 32 * run)


def norm_body(x_ref, gain_ref, order_ref, *refs):
    out_ref = refs[-1]
    x = x_ref[...].astype(F32)
    rows = x.shape[0]
    mean = jnp.mean(x * x, axis=-1, keepdims=True)
    normed = (x * lax.rsqrt(mean + 1e-06) * gain_ref[...]).astype(BF16)
    k = order_ref.shape[0]
    blocks = jnp.concatenate([normed[:, y * k : (y + 1) * k] for y in range(4)], 0)
    moved = dot(blocks, order_ref[...]).astype(BF16)
    for y in range(4):
        out_ref[:, y * k : (y + 1) * k] = moved[y * rows : (y + 1) * rows]


def norm_ordered(x, gain, order, total, block, at, into=()):
    rows, width = x.shape
    return pl.pallas_call(
        norm_body,
        grid=(rows // block,),
        in_specs=[
            pl.BlockSpec((block, width), lambda i: (i, 0)),
            pl.BlockSpec((1, width), lambda i: (0, 0)),
            pl.BlockSpec(order.shape, lambda i: (0, 0)),
        ]
        + [pl.BlockSpec(memory_space=pl.ANY)] * len(into),
        out_specs=pl.BlockSpec((block, width), lambda i: (at + i, 0)),
        out_shape=jax.ShapeDtypeStruct((total, width), BF16),
        input_output_aliases={3 + i: i for i in range(len(into))},
        compiler_params=params(24, "arbitrary"),
        cost_estimate=pl.CostEstimate(
            flops=2 * rows * width * 640, bytes_accessed=4 * rows * width, transcendentals=0
        ),
        name="norm_ordered",
    )(x, gain[None], order, *into)


def rotate(v, cos_ref, sin_ref):
    half = v[:, :128]
    turned = half * cos_ref[...] + pltpu.roll(half, 64, 1) * sin_ref[...]
    return jnp.concatenate([turned, v[:, 128:]], 1)


def project_body(rows, x_ref, w_ref, cos_ref, sin_ref, ours_ref, other_ref):
    extra = ours_ref.shape[1] - rows
    made = rotate(dot(x_ref[...], w_ref[...]), cos_ref.at[0], sin_ref.at[0]).astype(BF16)
    ours_ref[0, :rows] = made[:rows]
    other_ref[0, :rows] = made[rows : 2 * rows]
    ours_ref[0, rows:] = made[2 * rows : 2 * rows + extra]
    other_ref[0, rows:] = made[2 * rows + extra :]


def project(first, count, rows, x, w, cos, sin, hd):
    total, depth = x.shape
    last = w.shape[1] // hd - 1
    shape = jax.ShapeDtypeStruct((count, total // 2, hd), BF16)
    table = pl.BlockSpec((1, total, 128), lambda i: ((first + i) // last, 0, 0))
    return pl.pallas_call(
        functools.partial(project_body, rows),
        grid=(count,),
        in_specs=[
            pl.BlockSpec((total, depth), lambda i: (0, 0)),
            pl.BlockSpec((depth, hd), lambda i: (0, first + i)),
            table,
            table,
        ],
        out_specs=[pl.BlockSpec((1, total // 2, hd), lambda i: (i, 0, 0))] * 2,
        out_shape=[shape, shape],
        compiler_params=params(32, "arbitrary"),
        cost_estimate=pl.CostEstimate(
            flops=2 * total * count * depth * hd,
            bytes_accessed=2 * count * depth * hd,
            transcendentals=0,
        ),
        name="project",
    )(x, w, cos, sin)


SLAB = 24


def decode_body(
    info_ref, oab_ref, oc_ref, tab_ref, tc_ref, own_ref, cache_ref, out_ref, gather_ref, spill_ref
):
    i = pl.program_id(0)
    length, to, core = info_ref[i], info_ref[2 + i], info_ref[4]
    hd = cache_ref.shape[2] // 2
    window = cache_ref.shape[1]
    for half, (ab_ref, c_ref) in enumerate(((oab_ref, oc_ref), (tab_ref, tc_ref))):
        for h in range(5):
            block = ab_ref[h] if h < 4 else c_ref[0]
            block = block.astype(F32)
            row = jnp.where(i == 0, block[0:1], block[1:2])
            gather_ref[half * 5 + h : half * 5 + h + 1] = row
    gather_ref[10:16] = jnp.zeros((6, hd), F32)
    q = gather_ref[...].astype(BF16)
    scores = dot_t(q, cache_ref[0, :, :hd])
    own_row = own_ref[...].astype(F32)
    own_row = jnp.where(i == 0, own_row[0:1], own_row[1:2])
    own = jnp.sum(gather_ref[...] * own_row[:, :hd], axis=1, keepdims=True)
    slot = lax.broadcasted_iota(jnp.int32, scores.shape, 1)
    met = (slot < length) & (slot != lax.rem(length, window))
    scores = jnp.where(met, scores, NEG)
    top = jnp.maximum(jnp.max(scores, 1, keepdims=True), own)
    scale = LOG2E * hd**-0.5
    terms = jnp.where(met, jnp.exp2((scores - top) * scale), 0.0)
    own_term = jnp.exp2((own - top) * scale)
    total = jnp.sum(terms, 1, keepdims=True) + own_term
    weights = (terms / total).astype(BF16)
    own_weight = (own_term / total).astype(BF16).astype(F32)
    mixed = dot(weights, cache_ref[0, :, hd:]) + own_weight * own_row[:, hd:]
    spill_ref[20:] = jnp.zeros((SLAB - 20, 128), F32)
    for h in range(10):
        head = jnp.where(core == 0, h, (h + 5) % 10)
        for part in range(2):
            spill_ref[pl.ds(2 * head + part, 1)] = mixed[h : h + 1, part * 128 : part * 128 + 128]
    out_ref[to] = spill_ref[...].astype(BF16)


def decode_attend(info, parts, own, cache, places):
    n, window, wide = cache.shape
    hd = wide // 2
    last = parts[0].shape[1] // EXTRA - 1
    return pl.pallas_call(
        decode_body,
        grid_spec=pltpu.PrefetchScalarGridSpec(
            num_scalar_prefetch=1,
            grid=(n,),
            in_specs=[
                pl.BlockSpec((p.shape[0], EXTRA, hd), lambda i, s: (0, last, 0)) for p in parts
            ]
            + [
                pl.BlockSpec((EXTRA, wide), lambda i, s: (last, 0)),
                pl.BlockSpec((1, window, wide), lambda i, s: (i, 0, 0)),
            ],
            out_specs=pl.BlockSpec((places, SLAB, 128), lambda i, s: (0, 0, 0)),
            scratch_shapes=[pltpu.VMEM((16, hd), F32), pltpu.VMEM((SLAB, 128), F32)],
        ),
        out_shape=jax.ShapeDtypeStruct((places, SLAB, 128), BF16),
        compiler_params=params(24, "arbitrary"),
        cost_estimate=pl.CostEstimate(
            flops=64 * n * hd * window, bytes_accessed=4 * n * hd * window, transcendentals=0
        ),
        name="decode_attend",
    )(info, *parts, own, cache)


def interleave_body(z_ref, *refs):
    pieces, out_ref = refs[:4], refs[4]
    run = pieces[0].shape[0] // 2
    for z in range(4):

        @pl.when(z_ref[0] == z)
        def _():
            for core in range(2):
                rows = [
                    pieces[(z - at) % 4][core * run : (core + 1) * run].astype(F32) for at in range(4)
                ]
                out_ref[core] = jnp.concatenate(rows, 0).astype(BF16)


def interleave(z, pieces):
    rows, cols = pieces[0].shape
    vmem = pl.BlockSpec(memory_space=pltpu.VMEM)
    return pl.pallas_call(
        interleave_body,
        in_specs=[pl.BlockSpec(memory_space=pltpu.SMEM)] + [vmem] * 4,
        out_specs=vmem,
        out_shape=jax.ShapeDtypeStruct((2, 2 * rows, cols), BF16),
        compiler_params=params(8),
        name="interleave",
    )(z, *pieces)


def place_body(slot_ref, here_ref, rows_ref, out_ref):
    here = here_ref[0]
    for i in range(rows_ref.shape[0]):
        core, z, each = i // 8, i // 2 % 4, i % 2
        source = (here & 0b1101100) | (core * 16 + z)
        slot = slot_ref[source * 2 + each]
        to = slot >> 1

        @pl.when((to & 0b0010011) == (here & 0b0010011))
        def _():
            chip = ((to >> 5) << 2) | ((to >> 2) & 3)
            out_ref[chip * 2 + (slot & 1)] = rows_ref[i]


def place(slots, here, rows):
    smem = pl.BlockSpec(memory_space=pltpu.SMEM)
    vmem = pl.BlockSpec(memory_space=pltpu.VMEM)
    return pl.pallas_call(
        place_body,
        in_specs=[smem, smem, vmem],
        out_specs=vmem,
        out_shape=jax.ShapeDtypeStruct((32,) + rows.shape[1:], BF16),
        compiler_params=params(8),
        name="place",
    )(slots, here, rows)


def pick_body(came_ref, slab_ref, out_ref):
    out_ref[...] = slab_ref[...]


def by_device(came):
    return came >> 1


def by_chip(came):
    return ((came >> 6) << 2) | ((came >> 3) & 3)


def pick(arrived, came_from, where):
    slab = arrived.shape[1:]
    return pl.pallas_call(
        pick_body,
        grid_spec=pltpu.PrefetchScalarGridSpec(
            num_scalar_prefetch=1,
            grid=(2,),
            in_specs=[
                pl.BlockSpec((1,) + slab, lambda i, s: (where(s[i]) * 2 + i, 0, 0))
            ],
            out_specs=pl.BlockSpec((1,) + slab, lambda i, s: (i, 0, 0)),
        ),
        out_shape=jax.ShapeDtypeStruct((2,) + slab, BF16),
        compiler_params=params(8, "arbitrary"),
        name="pick",
    )(came_from, arrived)


def span_body(index_ref, ab1_ref, c1_ref, ab2_ref, c2_ref, k_ref, v_ref, cache_ref, out_ref):
    index = index_ref[0]
    last = pl.program_id(0) == pl.num_programs(0) - 1
    rows, hd = k_ref.shape
    q = jnp.concatenate(
        [jnp.where(last, c1_ref[0], ab1_ref[0]), jnp.where(last, c2_ref[0], ab2_ref[0])], 0
    )
    both = 2 * rows
    blocks = cache_ref.shape[1] // rows
    wrapped = index >= blocks
    row = lax.rem(lax.broadcasted_iota(jnp.int32, (both, rows), 0), rows)
    col = lax.broadcasted_iota(jnp.int32, (both, rows), 1)
    own = col <= row
    starts, scores, shifts = [], [], []
    top = None
    for rel in range(blocks):
        block = lax.rem(index + rel, blocks)
        start = pl.multiple_of(block * rows, rows)
        starts.append(start)
        s = dot_t(q, cache_ref[0, pl.ds(start, rows), :hd])
        if rel == 0:
            s = jnp.where(own, dot_t(q, k_ref[...]), jnp.where(wrapped, s, NEG))
            shift = jnp.float32(0)
        else:
            shift = jnp.where(wrapped | (block < index), jnp.float32(0), jnp.float32(NEG))
        scores.append(s)
        shifts.append(shift)
        peak = jnp.max(s, 1, keepdims=True) + shift
        top = peak if top is None else jnp.maximum(top, peak)
    scale = LOG2E * hd**-0.5
    base = top * scale
    total = jnp.zeros((both, 1), F32)
    mixed = jnp.zeros((both, hd), F32)
    for rel in range(blocks):
        terms = jnp.exp2(scores[rel] * scale - (base - shifts[rel]))
        total += jnp.sum(terms, 1, keepdims=True)
        old_values = cache_ref[0, pl.ds(starts[rel], rows), hd:]
        if rel == 0:
            mixed += dot(jnp.where(own, terms, 0.0).astype(BF16), v_ref[...])
            mixed += dot(jnp.where(own, 0.0, terms).astype(BF16), old_values)
        else:
            mixed += dot(terms.astype(BF16), old_values)
    made = (mixed / total).astype(BF16)
    out_ref[0] = made[:rows]
    out_ref[1] = made[rows:]


def span_attend(index, ours, theirs, key, value, rows, cache):
    half, hd = ours[0].shape[0] + 1, ours[0].shape[2]
    heads = 2 * half
    window = cache.shape[1]
    many = pl.BlockSpec((1, rows, hd), lambda h, s: (jnp.minimum(h, half - 2), 0, 0))
    single = pl.BlockSpec((1, rows, hd), lambda h, s: (0, 0, 0))
    pair = pl.BlockSpec((rows, hd), lambda h, s: (0, 0))
    return pl.pallas_call(
        span_body,
        grid_spec=pltpu.PrefetchScalarGridSpec(
            num_scalar_prefetch=1,
            grid=(half,),
            in_specs=[many, single, many, single, pair, pair]
            + [pl.BlockSpec((1, window, 2 * hd), lambda h, s: (0, 0, 0))],
            out_specs=pl.BlockSpec((2, rows, hd), lambda h, s: (0, 0, h)),
        ),
        out_shape=jax.ShapeDtypeStruct((2, rows, half * hd), BF16),
        compiler_params=params(36, "arbitrary"),
        cost_estimate=pl.CostEstimate(
            flops=4 * heads * rows * hd * (window + rows),
            bytes_accessed=4 * hd * window,
            transcendentals=heads * rows * window,
        ),
        name="span_attend",
    )(index, *ours, *theirs, key, value, cache)


def finish_body(
    info_ref, att_ref, datt_ref, x_ref, dx_ref, *refs
):
    chunks, (out_ref, dout_ref, lhs, w, sem) = refs[:16], refs[16:]
    rows, k = att_ref.shape[1:]
    step = pl.program_id(0)
    core = info_ref[0]

    def copies(quarter):
        for i in range(4):
            place = info_ref[1 + quarter * 4 + i]
            if quarter % 2:
                to = w.at[quarter, place]
            else:
                to = w.at[quarter, :, :, place]
            yield pltpu.make_async_copy(chunks[quarter * 4 + i], to, sem.at[quarter, i])

    @pl.when(step == 0)
    def _():
        for quarter in range(4):
            for copy in copies(quarter):
                copy.start()
        lhs[core, :rows] = att_ref[0]
        lhs[1 - core, :rows] = att_ref[1]
        lhs[0, rows:] = datt_ref[:, :k]
        lhs[1, rows:] = datt_ref[:, k:]

    for quarter in range(4):

        @pl.when(step == quarter)
        def _():
            for copy in copies(quarter):
                copy.wait()

    total = None
    for half in range(2):
        right = w[step, 2 * half : 2 * half + 2].reshape(k, w.shape[-1])
        term = dot(lhs[half], right)
        total = term if total is None else total + term
    out_ref[...] = (x_ref[...].astype(F32) + total[:rows]).astype(BF16)
    drows = dx_ref.shape[0]
    dout_ref[...] = (dx_ref[...].astype(F32) + total[rows : rows + drows]).astype(BF16)


def finish(info, att, datt, x, dx, chunks):
    rows, n = x.shape
    drows = dx.shape[0]
    run, bn = chunks[0].shape[2:]

    def column(i, s):
        return 0, lax.rem(s[0] * 2 + i, 4)

    return pl.pallas_call(
        finish_body,
        grid_spec=pltpu.PrefetchScalarGridSpec(
            num_scalar_prefetch=1,
            grid=(4,),
            in_specs=[
                pl.BlockSpec(att.shape, lambda i, s: (0, 0, 0)),
                pl.BlockSpec(datt.shape, lambda i, s: (0, 0)),
                pl.BlockSpec((rows, bn), column),
                pl.BlockSpec((drows, bn), column),
            ]
            + [pl.BlockSpec(memory_space=pl.ANY)] * 16,
            out_specs=[pl.BlockSpec((rows, bn), column), pl.BlockSpec((drows, bn), column)],
            scratch_shapes=[
                pltpu.VMEM((2, rows + EXTRA, n // 2), BF16),
                pltpu.VMEM((4, 4, 2, 4, run, bn), BF16),
                pltpu.SemaphoreType.DMA((4, 4)),
            ],
        ),
        out_shape=[
            jax.ShapeDtypeStruct((rows, n), BF16),
            jax.ShapeDtypeStruct((drows, n), BF16),
        ],
        compiler_params=params(60, "arbitrary"),
        cost_estimate=pl.CostEstimate(
            flops=2 * rows * n * n, bytes_accessed=2 * n * n, transcendentals=0
        ),
        name="finish",
    )(info, att, datt, x, dx, *chunks)


def exchange(sent, axes):
    members = lax.axis_size(axes)
    got = lax.all_to_all(sent.reshape((members, -1) + sent.shape[1:]), axes, 0, 0)
    return got.reshape(sent.shape)


STRIDE = {"y": 32, "x": 4, "z": 1}
DEVICES = np.arange(128)


def spot(axis):
    return DEVICES // STRIDE[axis] % 4


def send(v, axis, by):
    at = spot(axis)
    to = DEVICES + ((at + by) % 4 - at) * STRIDE[axis]
    return lax.ppermute(v, AXES, list(zip(DEVICES.tolist(), to.tolist())))


def swap(v):
    return lax.ppermute(v, AXES, list(zip(DEVICES.tolist(), (DEVICES ^ 16).tolist())))


RING = np.where(DEVICES // 16 % 2 == 0, 1, 3)


def put(whole, piece, index, place):
    start = [jnp.uint32(0)] * whole.ndim
    start[place] = index
    return lax.dynamic_update_slice(whole, jnp.expand_dims(piece, place), start)


def shards(
    devices,
    span_tokens,
    decode_tokens,
    norm_gain,
    query_weight,
    keyval_weight,
    output_weight,
    span_cache,
    decode_cache,
    span_index,
    decode_length,
    cache_slot,
):
    rows, width = span_tokens.shape[1:]
    own = decode_cache.shape[0]
    hd = keyval_weight.shape[1] // 2
    device = lax.axis_index(AXES).astype(jnp.uint32)
    core = ((device >> 4) & 1).astype(jnp.int32)
    first_core = core == 0
    run = query_weight.shape[0]

    half_q, half_kv = width // 2, hd
    halves = [
        jnp.concatenate(
            [
                query_weight[:, i * half_q : (i + 1) * half_q],
                keyval_weight[:, i * half_kv : (i + 1) * half_kv],
                output_weight[:, i * half_q : (i + 1) * half_q],
            ],
            1,
        )
        for i in range(2)
    ]
    got = swap(jnp.where(first_core, halves[1], halves[0]))
    piece = jnp.where(
        first_core, jnp.concatenate([halves[0], got], 0), jnp.concatenate([got, halves[1]], 0)
    )
    places = devices * own
    slots_here = (device * own).astype(jnp.int32) + jnp.arange(own, dtype=jnp.int32)
    slot_of_mine = lax.dynamic_slice(cache_slot, (device * own,), (own,))
    request_of_mine = jnp.argmax(cache_slot[None, :] == slots_here[:, None], 1).astype(jnp.int32)
    digits = jnp.stack([decode_length // 256, decode_length % 256], 1).astype(BF16)
    tagged = jnp.concatenate([decode_tokens, jnp.pad(digits, ((0, 0), (0, 510)))], 1)
    tagged = tagged.reshape(own, SLAB, 128)
    tagged = jnp.broadcast_to(tagged, (8,) + tagged.shape).reshape(8 * own, SLAB, 128)
    split = half_q + half_kv
    first_weight = lax.all_gather(piece[:, :split], CHIPS, axis=0, tiled=True)

    here = {axis: (device >> shift) & 3 for axis, shift in (("y", 5), ("x", 2), ("z", 0))}
    back = 1 - 2 * ((device >> 4) & 1)
    came = {axis: [(at - back * k) & 3 for k in range(4)] for axis, at in here.items()}
    strip = piece[:, split:]
    strips = [strip] + [send(strip, "z", k) for k in (1, 2, 3)]
    tagged, _ = lax.optimization_barrier((tagged, strips))
    tagged = place(cache_slot, device.astype(jnp.int32)[None], exchange(tagged, ("c", "z")))
    strips = interleave(here["z"].astype(jnp.int32)[None], strips)
    bn = half_q // 2
    stack = [strips[:, :, :bn], strips[:, :, bn:]]
    plan = (("y", 0, "x", 2), ("x", 1, "y", 0))
    parts = [
        jnp.zeros((4, 2, 4 * run, bn), BF16),
        jnp.zeros((2, 4, 4 * run, bn), BF16),
    ]
    for k in range(4):
        for i, (axis, dim, _, _) in enumerate(plan):
            stack[i] = send(stack[i], axis, RING) if k else stack[i]
            parts[i] = put(parts[i], stack[i], came[axis][k], dim)
    arrived = pick(exchange(tagged, ("y", "x")), request_of_mine, by_chip)
    arrived = arrived.reshape(own, SLAB * 128)
    own_tokens = jnp.pad(arrived[:, :width], ((0, EXTRA - own), (0, 0)))
    tags = arrived[:, width : width + 2].astype(jnp.int32)
    own_length = tags[:, 0] * 256 + tags[:, 1]

    offset = span_index[0] * rows
    span_positions = offset + jnp.arange(rows, dtype=jnp.int32)
    decode_positions = jnp.pad(own_length, (0, EXTRA - own))
    positions = jnp.concatenate(
        [span_positions, swap(span_positions), decode_positions, swap(decode_positions)]
    )
    quarter = hd // 4
    frequency = 10000.0 ** (-jnp.arange(quarter, dtype=F32) / quarter)
    angles = positions.astype(F32)[:, None] * frequency
    cos, sin = jnp.cos(angles), jnp.sin(angles)
    cos = jnp.concatenate([cos, cos], 1)
    sin = jnp.concatenate([-sin, sin], 1)
    cos = jnp.stack([cos, jnp.where(first_core, cos, 1.0)])
    sin = jnp.stack([sin, jnp.where(first_core, sin, 0.0)])

    order = arrival_order(run)
    both_spans = jnp.concatenate([span_tokens[0], swap(span_tokens[0])], 0)
    both_decodes = jnp.concatenate([own_tokens, swap(own_tokens)], 0)
    total = 2 * (rows + EXTRA)
    lhs = norm_ordered(both_spans, norm_gain, order, total, 128, 0)
    at = 2 * rows // (2 * EXTRA)
    lhs = norm_ordered(both_decodes, norm_gain, order, total, 2 * EXTRA, at, (lhs,))
    mine = [[part] for part in parts]
    theirs = [[swap(part)] for part in parts]
    def ring_step(parts):
        parts = [send(part, p[2], RING) for part, p in zip(parts, plan)]
        for i in range(2):
            mine[i].append(parts[i])
        return parts

    def swap_last(after):
        parts, _ = lax.optimization_barrier(([m[-1] for m in mine], after))
        for i in range(2):
            theirs[i].append(swap(parts[i]))

    parts = ring_step(parts)
    swap_last(())
    shifts = jnp.asarray([2] * 4 + [5] * 4 + [2] * 4 + [5] * 4, jnp.int32)
    steps = jnp.asarray([0, 1, 2, 3] * 2 + [0, -1, -2, -3] * 2, jnp.int32)
    came_from = (((device.astype(jnp.int32) >> shifts) & 3) - (1 - 2 * core) * steps) & 3
    finish_info = jnp.concatenate([core[None], came_from])
    info = jnp.concatenate([own_length, request_of_mine, core[None]])
    parts, lhs, cos, sin, finish_info, info = lax.optimization_barrier(
        (parts, lhs, cos, sin, finish_info, info)
    )
    ring_step(parts)
    first_weight, cos, sin = (
        pltpu.with_memory_space_constraint(v, pltpu.HBM) for v in (first_weight, cos, sin)
    )
    ours_c, other_c = project(4, 2, rows, lhs, first_weight, cos, sin, hd)
    theirs_c = swap(other_c)
    ours_ab, other_ab = project(0, 4, rows, lhs, first_weight, cos, sin, hd)
    theirs_ab = swap(other_ab)

    key = jnp.where(first_core, ours_c[1], theirs_c[1])
    value = jnp.where(first_core, theirs_c[1], ours_c[1])
    keyval = jnp.concatenate([key, value], 1)
    decode_keyval = keyval[rows : rows + own]
    quarters = (ours_ab, ours_c, theirs_ab, theirs_c)
    routed = decode_attend(info, quarters, keyval, decode_cache, places)
    home = exchange(routed, AXES)
    swap_last(routed)
    parts, _ = lax.optimization_barrier(([m[-1] for m in mine], routed))
    ring_step(parts)
    att = span_attend(
        span_index, (ours_ab, ours_c), (theirs_ab, theirs_c), key, value, rows, span_cache
    )
    swap_last(att)
    home = pick(home, slot_of_mine, by_device).reshape(own, SLAB * 128)[:, :width]
    span_output, decode_output = finish(
        finish_info,
        att,
        jnp.pad(home, ((0, EXTRA - own), (0, 0))),
        span_tokens[0],
        decode_tokens,
        [c for half in (mine, theirs) for part in half for c in part],
    )
    return span_output[None], keyval[:rows][None], decode_output, decode_keyval


def solution(mesh):
    both = P(AXES)
    return jax.shard_map(
        functools.partial(shards, mesh.size),
        mesh=Mesh(mesh.devices.reshape(4, 2, 4, 4), AXES),
        in_specs=(both, both, P(), both, both, both, both, both, both, both, P()),
        out_specs=(both, both, both, both),
        check_vma=False,
    )
```
